32 devices in a mesh: harm: 4 (over z), blk: 8 (over y, x, core).
Axes of the slice: x: 2, y: 2, z: 4, core: 2. Of those that a mesh axis runs over, the one named last changes fastest.
Arguments:
- source: float32 [48, 10, 128, 128], P('harm', None, 'blk'), may hold values from -8 to 8
- diag_shift: float32 [128, 128], P('blk'), may hold values from 0.5 to 2.5
- coupling: float32 [48, 10, 10], P('harm'), may hold values from -0.5 to 0.5
- sweep_gain: float32 [48, 10, 10], P('harm')
- gust_field: float32 [48, 10, 128], P('harm', None, 'blk'), may hold values from -6 to 6
- gust_mixing: float32 [48, 48], P('harm'), may hold values from -0.875 to 0.875
- mode_orders: int32 [48, 32], P('harm'), may hold values from -32 to 31
- cut_on_count: int32 [48], P('harm'), may hold values from 1 to 32, 768 in all
Outputs:
- solution: float32 [48, 10, 128, 128], P('harm', None, 'blk')
- duct_modes: float32 [48, 2, 32], P('harm', None, 'blk')
The draws below stay inside these ranges and needn't reach their ends.
Inputs may be any that keep to these rules, and one draw needn't show every extreme that they name: `cut_on_count`: the counts of all harmonics sum to 768.
All inputs are finite; a program needn't handle non-finite values. No bound on the sum of `cut_on_count` on one device may be relied on, other than what follows from the above.
Results may differ from the reference program's by a relative error of at most 0.0003.
Values sent between devices are 32-bit elements; how exact they have to be, the bound alone decides.
No kernel may reach another device: no remote copies, remote signals or barrier semaphores. Data moves between devices by JAX's collectives and lax.ppermute only.
A program may use at most 128 MiB of HBM per device.

```python
import math
import jax
import jax.numpy as jnp
import numpy as np
from jax import lax

CX = 128
KRYLOV = 6
SWEEPS = 3
KMAX = 32
HARM = 48
NY = 128


def draw_sweep_gain(key, part):
    first_key, second_key = jax.random.split(key)
    identity = jnp.eye(10, dtype=jnp.float32)
    diagonal = jax.random.uniform(first_key, (HARM, 10), jnp.float32, 0.12, 0.2)
    offdiag = 0.012 * jax.random.normal(second_key, (HARM, 10, 10), jnp.float32)
    return offdiag * (1.0 - identity[None]) + identity[None] * diagonal[:, :, None]


def with_ends(result, key, low, top_value):
    extent = result.shape
    index_at = [jax.random.randint(jax.random.fold_in(key, axis), (), 0, extent[axis]) for axis in range(len(extent))]
    result = result.at[tuple(index_at)].set(low)
    longest = extent.index(max(extent))
    index_at[longest] = (index_at[longest] + 1) % extent[longest]
    return result.at[tuple(index_at)].set(top_value)


def block_levels(key, extent, cuts, low, high):
    factor_of, own = 1.0, jax.random.fold_in(key, 6)
    for position, shards_of in cuts:
        heights = jnp.exp(jax.random.uniform(jax.random.fold_in(own, position), (shards_of,), jnp.float32, low / len(cuts), high / len(cuts)))
        factor_of = factor_of * jnp.repeat(heights, extent[position] // shards_of).reshape([-1 if axis == position else 1 for axis in range(len(extent))])
    return factor_of


def length_profile(number_of, total, bound, slope):
    portions = [(1 << 20) // math.isqrt(rank ** slope) + 1 for rank in range(2, number_of + 1)]
    surplus, counts = total - bound - (number_of - 1), [1] * (number_of - 1)
    while surplus > 0:
        movable = [i for i in range(number_of - 1) if counts[i] < bound]
        whole, budget = sum([portions[i] for i in movable]), surplus
        for i in movable:
            extra = min(bound - counts[i], max(1, budget * portions[i] // whole), surplus)
            counts[i] = counts[i] + extra
            surplus = surplus - extra
    return np.array([bound] + counts)


def uneven_parts(key, amount, total, bound, lean):
    if amount == 2:
        one = jax.random.randint(key, (), max(1, total - bound), min(bound, total - 1) + 1)
        return jnp.stack([one, total - one])
    sizes = jnp.asarray(length_profile(amount, total, bound, lean), jnp.int32)
    couples = (amount - 1) // 2
    giver, receiver = sizes[1:1 + 2 * couples:2], sizes[2:2 + 2 * couples:2]
    margin = jnp.minimum(giver - 1, bound - receiver)
    shifted = jax.random.randint(jax.random.fold_in(key, 1), (couples,), 0, 1 << 20) % (margin + 1)
    sizes = sizes.at[1:1 + 2 * couples:2].set(giver - shifted).at[2:2 + 2 * couples:2].set(receiver + shifted)
    return sizes[jax.random.permutation(jax.random.fold_in(key, 2), amount)]


def scatter_about(stream_key, shape, deviation, most, cuts=(), held_as=jnp.bfloat16):
    result = deviation * jax.random.normal(stream_key, shape, jnp.float32)
    if cuts:
        result = result * block_levels(stream_key, shape, cuts, -0.22, 0.18)
    return jnp.clip(result, -most, most).astype(held_as)


def setup_inputs(seed: int = 0) -> dict:
    key_list = jax.random.split(jax.random.key(seed), 9)
    source = scatter_about(key_list[0], (HARM, 10, NY, CX), 1.0, 8.0, ((0, 4), (2, 8)), jnp.float32)
    diag_shift = jnp.clip(0.5 + 2.0 * jax.random.uniform(key_list[1], (NY, CX), jnp.float32) ** block_levels(key_list[1], (NY, CX), ((0, 8),), -0.2, 0.2), 0.5, 2.5)
    coupling = scatter_about(key_list[2], (HARM, 10, 10), 0.1, 0.5, ((0, 4),), jnp.float32)
    sweep_gain = draw_sweep_gain(jax.random.fold_in(key_list[8], 71), 0)
    gust_field = scatter_about(key_list[4], (HARM, 10, NY), 1.0, 6.0, ((0, 4), (2, 8)), jnp.float32)
    gust_mixing = scatter_about(key_list[5], (HARM, HARM), HARM ** -0.5, 0.875, ((0, 4),), jnp.float32)
    mode_orders = with_ends(jax.random.randint(key_list[6], (HARM, KMAX), 0 - NY // 4, NY // 4), jax.random.fold_in(key_list[6], 1), 0 - NY // 4, (NY // 4) - 1).astype(jnp.int32)
    cut_on_count = uneven_parts(key_list[7], HARM, KMAX // 2 * HARM, KMAX, 2).astype(jnp.int32)
    return dict(source=source, diag_shift=diag_shift, coupling=coupling, sweep_gain=sweep_gain, gust_field=gust_field, gust_mixing=gust_mixing, mode_orders=mode_orders, cut_on_count=cut_on_count)


precise = lax.Precision.HIGHEST

def streamwise_upwind(state_vec):
    return jnp.concatenate([jnp.zeros_like(state_vec[..., :1]), state_vec[..., :-1]], axis=-1)

def operate(state_vec, diag_shift, coupling_h):
    lateral = jnp.roll(state_vec, 1, axis=1) + jnp.roll(state_vec, -1, axis=1)
    mixed_part = jnp.einsum('cd,dyx->cyx', coupling_h, state_vec, precision=precise)
    return (4.0 + diag_shift) * state_vec + mixed_part - streamwise_upwind(state_vec) - 1.5 * lateral

def solve_normal(normal, right_side):
    factor_low = jnp.linalg.cholesky(normal)
    dimension = normal.shape[-1]
    forward = []
    for i in range(dimension):
        running = right_side[..., i]
        for k in range(i):
            running = running - factor_low[..., i, k] * forward[k]
        forward.append(running / factor_low[..., i, i])
    backward = [None] * dimension
    for i in range(dimension - 1, -1, -1):
        running = forward[i]
        for k in range(i + 1, dimension):
            running = running - factor_low[..., k, i] * backward[k]
        backward[i] = running / factor_low[..., i, i]
    return backward

def project_modes(trace_re, trace_im, orders, pitch_index, pitch_total):
    remainder = orders[:, :, None] * pitch_index[None, None, :] % pitch_total
    angles = 2.0 * math.pi / pitch_total * remainder.astype(jnp.float32)
    cosine_part = jnp.cos(angles)
    sine_part = jnp.sin(angles)
    wave_re = lax.optimization_barrier(jnp.sum(trace_re[:, None, :] * cosine_part + trace_im[:, None, :] * sine_part, axis=2))
    wave_im = lax.optimization_barrier(jnp.sum(trace_im[:, None, :] * cosine_part - trace_re[:, None, :] * sine_part, axis=2))
    return jnp.stack([wave_re, wave_im], axis=1)

def reference(source, diag_shift, coupling, sweep_gain, gust_field, gust_mixing, mode_orders, cut_on_count):
    inlet_term = jnp.einsum('hg,gcy->hcy', gust_mixing, gust_field, precision=precise)
    right_all = source.at[:, :, :, 0].add(inlet_term)

    def solve_one(packed):
        right_side, coupling_h, gain_h = packed

        def apply_gain(vector):
            return jnp.einsum('cd,dyx->cyx', gain_h, vector, precision=precise)
        beta_norm = jnp.sqrt(jnp.sum(right_side * right_side) + 1e-06)
        krylov_basis = [right_side / beta_norm]
        directions = []
        columns = []
        for j in range(KRYLOV):
            vector = krylov_basis[j]
            precond_vec = apply_gain(vector)
            for sweep_done in range(SWEEPS - 1):
                precond_vec = precond_vec + apply_gain(vector - operate(precond_vec, diag_shift, coupling_h))
            work_vec = operate(precond_vec, diag_shift, coupling_h)
            entries = []
            for i in range(j + 1):
                projected = jnp.sum(work_vec * krylov_basis[i])
                entries.append(projected)
                work_vec = work_vec - projected * krylov_basis[i]
            length = jnp.sqrt(jnp.sum(work_vec * work_vec) + 1e-06)
            entries.append(length)
            if j + 1 < KRYLOV:
                krylov_basis.append(work_vec / length)
            directions.append(precond_vec)
            columns.append(jnp.stack(entries + [jnp.zeros_like(length)] * (KRYLOV - j - 1)))
        hessenberg = jnp.stack(columns, axis=1)
        normal = jnp.dot(hessenberg.T, hessenberg, precision=precise)
        coeffs = solve_normal(normal, beta_norm * hessenberg[0, :])
        solution_h = coeffs[0] * directions[0]
        for j in range(1, KRYLOV):
            solution_h = solution_h + coeffs[j] * directions[j]
        return solution_h
    solution = lax.map(solve_one, (right_all, coupling, sweep_gain))
    trace_re = solution[:, 8, :, -1] + solution[:, 2, :, -1]
    trace_im = solution[:, 9, :, -1] + solution[:, 3, :, -1]
    wave_sums = project_modes(trace_re, trace_im, mode_orders, jnp.arange(NY, dtype=jnp.int32), NY)
    live_slots = jnp.arange(KMAX, dtype=jnp.int32)[None, :] < cut_on_count[:, None]
    duct_modes = jnp.where(live_slots[:, None, :], wave_sums * (1.0 / math.sqrt(NY)), 0.0)
    return (solution, duct_modes)
```

```python
import functools
import math

import jax
import jax.numpy as jnp
from jax import lax
from jax.experimental import pallas as pl
from jax.experimental.pallas import tpu as pltpu
from jax.sharding import PartitionSpec as P

KRYLOV = 6
COMPS = 10
SUB = 8
ROWS = COMPS * SUB
EPS = 1e-06

precise = lax.Precision.HIGHEST
f32, bf16 = jnp.float32, jnp.bfloat16


def rows_by_group(entries, copies):
    wide = copies * ROWS
    row_of = lax.broadcasted_iota(jnp.int32, (ROWS, COMPS), 0) // SUB
    pick_rows = (row_of == lax.broadcasted_iota(jnp.int32, (ROWS, COMPS), 1)).astype(f32)
    column_of = (lax.broadcasted_iota(jnp.int32, (COMPS, wide), 1) % ROWS) // SUB
    pick_columns = (column_of == lax.broadcasted_iota(jnp.int32, (COMPS, wide), 0)).astype(f32)
    spread = jnp.dot(pick_rows, entries, precision=precise, preferred_element_type=f32)
    spread = jnp.dot(spread, pick_columns, precision=precise, preferred_element_type=f32)
    same = (lax.broadcasted_iota(jnp.int32, (ROWS, wide), 0) % SUB) == (
        lax.broadcasted_iota(jnp.int32, (ROWS, wide), 1) % SUB
    )
    return jnp.where(same, spread, 0.0)


def split_matrix(entries):
    full = rows_by_group(entries, 3)
    high = full.astype(bf16)
    low = (full - high.astype(f32)).astype(bf16)
    column = lax.broadcasted_iota(jnp.int32, (ROWS, 3 * ROWS), 1)
    return jnp.where(column < 2 * ROWS, high.astype(f32), low.astype(f32)).astype(bf16)


def split_field(plane):
    high = plane.astype(bf16)
    low = (plane - high.astype(f32)).astype(bf16)
    return [high, low, high]


def solve_kernel(
    groups, in_rows, out_rows, slots,
    count_ref, in_ref, gain_ref, coupling_ref, cos_ref, sin_ref,
    out_ref,
    basis, direction, first, second, diag, trace_re, trace_im, gain_mat, step_mat, coupling_mat,
):
    length = diag.shape[0]
    block = 16
    stride = (groups // SUB) * in_rows
    out_stride = (groups // SUB) * out_rows
    gain, coupling = gain_ref[...], coupling_ref[...]
    gain_mat[...] = split_matrix(gain)
    step_mat[:, : 3 * ROWS] = split_matrix(gain)
    product = jnp.dot(gain, coupling, precision=precise, preferred_element_type=f32)
    step_mat[:, 3 * ROWS :] = split_matrix(product)
    coupling_mat[...] = split_matrix(coupling)
    inner = lax.broadcasted_iota(jnp.int32, (ROWS, 128), 1) > 0

    def total(acc):
        return jnp.sum(acc, axis=(0, 1), keepdims=True)

    def spread(scalar):
        return jnp.broadcast_to(scalar, (SUB, 128))

    def scaled(value, plane):
        return (plane.reshape(COMPS, SUB, 128) * value[None]).reshape(ROWS, 128)

    def fold(plane):
        return jnp.sum(plane.reshape(COMPS, SUB, 128), axis=0)

    def take(l, acc):
        start = (l // block) * in_rows + l % block
        planes = []
        for c in range(COMPS):
            piece = in_ref[pl.ds(start + c * block, SUB, stride=stride), :]
            planes.append(piece)
        plane = jnp.concatenate(planes, axis=0)
        basis[0, l] = plane
        diag[l] = 4.0 + in_ref[pl.ds(start + COMPS * block, SUB, stride=stride), :]
        return acc + fold(plane * plane)

    def wrap(field):
        for c in range(COMPS):
            rows = slice(c * SUB, (c + 1) * SUB)
            field[0, rows, :] = pltpu.roll(field[length, rows, :], 1, axis=0)
            field[length + 1, rows, :] = pltpu.roll(field[1, rows, :], SUB - 1, axis=0)

    def multiply(matrix, left, right):
        return jnp.dot(
            matrix[...],
            jnp.concatenate(
                [jnp.concatenate(left, axis=0), jnp.concatenate(right, axis=0)], axis=1
            ),
            preferred_element_type=f32,
        )

    def uncoupled(before, plane, after, diagonal):
        upwind = jnp.where(inner, pltpu.roll(plane, 1, axis=1), 0.0)
        return scaled(diagonal, plane) - upwind - 1.5 * (before + after)

    def window(field, l):
        planes = [field[l + i] for i in range(4)]
        terms = [
            uncoupled(planes[i], planes[i + 1], planes[i + 2], diag[l + i]) for i in range(2)
        ]
        return planes[1:3], terms

    acc = lax.fori_loop(0, length, take, jnp.zeros((SUB, 128), f32))
    squares = total(acc)
    beta = jnp.sqrt(squares + EPS)
    norms = [beta]
    lack = [EPS / (squares + EPS)]
    gram = {}
    hess = {}
    zero = jnp.zeros((SUB, 128), f32)

    for j in range(KRYLOV):
        inverse = spread(1.0 / norms[j])
        found = direction.at[j]

        def start_step(p, carry, j=j, inverse=inverse):
            l = 2 * p
            planes = [scaled(inverse, basis[j, l + i]) for i in range(2)]
            for i in range(2):
                basis[j, l + i] = planes[i]
            result = multiply(gain_mat, split_field(planes[0]), split_field(planes[1]))
            for i in range(2):
                first[l + i + 1] = result[:, 128 * i : 128 * (i + 1)]
            return carry

        lax.fori_loop(0, length // 2, start_step, 0)
        wrap(first)

        def sweep_one(p, carry):
            l = 2 * p
            planes, terms = window(first, l)
            result = multiply(
                step_mat,
                split_field(terms[0]) + split_field(planes[0]),
                split_field(terms[1]) + split_field(planes[1]),
            )
            for i in range(2):
                second[l + i + 1] = 2.0 * planes[i] - result[:, 128 * i : 128 * (i + 1)]
            return carry

        lax.fori_loop(0, length // 2, sweep_one, 0)
        wrap(second)

        def sweep_two(p, carry, found=found):
            l = 2 * p
            planes, terms = window(second, l)
            result = multiply(
                step_mat,
                split_field(terms[0]) + split_field(planes[0]),
                split_field(terms[1]) + split_field(planes[1]),
            )
            for i in range(2):
                found[l + i + 1] = (
                    planes[i] + first[l + i + 1] - result[:, 128 * i : 128 * (i + 1)]
                )
            return carry

        lax.fori_loop(0, length // 2, sweep_two, 0)
        wrap(found)

        def apply_operator(p, accs, j=j, found=found):
            l = 2 * p
            planes, terms = window(found, l)
            result = multiply(coupling_mat, split_field(planes[0]), split_field(planes[1]))
            for i in range(2):
                work = terms[i] + result[:, 128 * i : 128 * (i + 1)]
                basis[j + 1, l + i] = work
                accs = tuple(
                    accs[k] + fold(work * basis[k, l + i]) for k in range(j + 1)
                )
            return accs

        accs = lax.fori_loop(0, length // 2, apply_operator, (zero,) * (j + 1))
        dots = [total(acc) for acc in accs]
        for i in range(j + 1):
            entry = dots[i]
            for k in range(i):
                entry = entry - hess[k, j] * gram[k, i]
            hess[i, j] = entry
        factors = [spread(hess[i, j]) for i in range(j + 1)]

        def orthogonalize(p, acc, j=j, factors=factors):
            for i in range(2):
                l = 2 * p + i
                work = basis[j + 1, l]
                for k in range(j + 1):
                    work = work - scaled(factors[k], basis[k, l])
                basis[j + 1, l] = work
                acc = acc + fold(work * work)
            return acc

        squares = total(lax.fori_loop(0, length // 2, orthogonalize, zero))
        size = jnp.sqrt(squares + EPS)
        hess[j + 1, j] = size
        norms.append(size)
        lack.append(EPS / (squares + EPS))
        for k in range(j + 1):
            entry = hess[k, j] * lack[k]
            for i in range(k + 1, j + 1):
                entry = entry - hess[i, j] * gram[k, i]
            gram[k, j + 1] = entry / size

    normal = {}
    for a in range(KRYLOV):
        for b in range(a + 1):
            value = hess[0, a] * hess[0, b]
            for k in range(1, b + 2):
                value = value + hess[k, a] * hess[k, b]
            normal[a, b] = value
    low = {}
    inverse_of = {}
    for a in range(KRYLOV):
        for b in range(a + 1):
            value = normal[a, b]
            for k in range(b):
                value = value - low[a, k] * low[b, k]
            if a == b:
                low[a, a] = jnp.sqrt(value)
                inverse_of[a] = 1.0 / low[a, a]
            else:
                low[a, b] = value * inverse_of[b]
    forward = []
    for a in range(KRYLOV):
        value = beta * hess[0, a]
        for k in range(a):
            value = value - low[a, k] * forward[k]
        forward.append(value * inverse_of[a])
    coeffs = [None] * KRYLOV
    for a in range(KRYLOV - 1, -1, -1):
        value = forward[a]
        for k in range(a + 1, KRYLOV):
            value = value - low[k, a] * coeffs[k]
        coeffs[a] = value * inverse_of[a]
    weights = [spread(c) for c in coeffs]

    def combine(l, carry):
        plane = scaled(weights[0], direction[0, l + 1])
        for j in range(1, KRYLOV):
            plane = plane + scaled(weights[j], direction[j, l + 1])
        start = (l // block) * out_rows + l % block
        pieces = [plane[c * SUB : (c + 1) * SUB, :] for c in range(COMPS)]
        for c in range(COMPS):
            out_ref[pl.ds(start + c * block, SUB, stride=out_stride), :] = pieces[c]
        trace_re[l] = pieces[8] + pieces[2]
        trace_im[l] = pieces[9] + pieces[3]
        return carry

    lax.fori_loop(0, length, combine, 0)

    full_re = trace_re[...].reshape(length * SUB, 128)
    full_im = trace_im[...].reshape(length * SUB, 128)
    cosine, sine = cos_ref[...], sin_ref[...]
    mix = functools.partial(jnp.dot, precision=precise, preferred_element_type=f32)
    live = lax.broadcasted_iota(jnp.int32, (cosine.shape[0], 128), 0) < count_ref[0]
    norm = 1.0 / math.sqrt(length * SUB)
    wave_re = jnp.where(live, (mix(cosine, full_re) + mix(sine, full_im)) * norm, 0.0)
    wave_im = jnp.where(live, (mix(cosine, full_im) - mix(sine, full_re)) * norm, 0.0)
    tail = COMPS * block
    for b in range(groups):
        at = b * out_rows + tail
        out_ref[at : at + out_rows - tail, :] = jnp.zeros((out_rows - tail, 128), f32)
        out_ref[at : at + slots, :] = wave_re[b * slots : (b + 1) * slots, :]
        out_ref[at + slots : at + 2 * slots, :] = wave_im[b * slots : (b + 1) * slots, :]


def solve(message, gain, coupling, orders, count, groups, pitch_local):
    pitch_total = groups * pitch_local
    length = pitch_total // SUB
    modes = orders.shape[0]
    slots = modes // groups
    in_rows = message.shape[1]
    out_rows = COMPS * pitch_local + -(-2 * slots // SUB) * SUB
    plane_order = jnp.arange(SUB)[None, :] * length + jnp.arange(length)[:, None]
    pitch_index = plane_order.reshape(-1).astype(jnp.int32)
    remainder = orders[:, None] * pitch_index[None, :] % pitch_total
    angles = 2.0 * math.pi / pitch_total * remainder.astype(f32)
    kernel = functools.partial(solve_kernel, groups, in_rows, out_rows, slots)
    in_vmem = pl.BlockSpec(memory_space=pltpu.VMEM)
    result = pl.pallas_call(
        kernel,
        out_shape=jax.ShapeDtypeStruct((groups * out_rows, 128), f32),
        in_specs=[pl.BlockSpec(memory_space=pltpu.SMEM)] + [in_vmem] * 5,
        out_specs=in_vmem,
        scratch_shapes=[
            pltpu.VMEM((KRYLOV + 1, length, ROWS, 128), f32),
            pltpu.VMEM((KRYLOV, length + 2, ROWS, 128), f32),
            pltpu.VMEM((length + 2, ROWS, 128), f32),
            pltpu.VMEM((length + 2, ROWS, 128), f32),
            pltpu.VMEM((length, SUB, 128), f32),
            pltpu.VMEM((length, SUB, 128), f32),
            pltpu.VMEM((length, SUB, 128), f32),
            pltpu.VMEM((ROWS, 3 * ROWS), bf16),
            pltpu.VMEM((ROWS, 6 * ROWS), bf16),
            pltpu.VMEM((ROWS, 3 * ROWS), bf16),
        ],
        compiler_params=pltpu.CompilerParams(vmem_limit_bytes=60 * 1024 * 1024),
    )(
        count.reshape(1),
        message.reshape(groups * in_rows, 128),
        gain,
        coupling,
        jnp.cos(angles),
        jnp.sin(angles),
    )
    return result.reshape(groups, out_rows, 128)


def local(
    source, diag_shift, coupling, sweep_gain, gust_field, gust_mixing, mode_orders, cut_on_count
):
    harmonics, comps, pitch_local, stream = source.shape
    groups = lax.axis_size("blk")
    me = lax.axis_index("blk")
    parts = lax.axis_size("harm")
    part = lax.axis_index("harm")

    inlet = jnp.zeros((harmonics, comps * pitch_local), f32)
    flat_gust = gust_field.reshape(harmonics, comps * pitch_local)
    for k in range(parts):
        block = flat_gust
        if k:
            block = lax.ppermute(flat_gust, "harm", [(i, (i + k) % parts) for i in range(parts)])
        origin = (part - k) % parts
        mixing = lax.dynamic_slice_in_dim(gust_mixing, origin * harmonics, harmonics, axis=1)
        inlet = inlet + jnp.dot(mixing, block, precision=precise)
    inlet = inlet.reshape(harmonics, comps, pitch_local)
    at_inlet = jnp.arange(stream) == 0
    right_side = source + jnp.where(at_inlet, inlet[..., None], 0.0)

    rounds = -(-harmonics // groups)
    diagonal = jnp.broadcast_to(diag_shift[None, None], (harmonics, 1, pitch_local, stream))
    message = jnp.concatenate([right_side, diagonal], axis=1)
    missing = rounds * groups - harmonics
    if missing:
        message = jnp.concatenate(
            [message, jnp.zeros((missing,) + message.shape[1:], f32)], axis=0
        )
    message = message.reshape(rounds * groups, -1, stream)

    solved = []
    for s in range(rounds):
        part_of = message[s * groups : (s + 1) * groups]
        arrived = lax.all_to_all(part_of, "blk", 0, 0, tiled=True)
        index = jnp.minimum(s * groups + me, harmonics - 1)
        pick = lambda array: lax.dynamic_index_in_dim(array, index, 0, keepdims=False)
        result = solve(
            arrived, pick(sweep_gain), pick(coupling), pick(mode_orders), pick(cut_on_count),
            groups, pitch_local,
        )
        solved.append(lax.all_to_all(result, "blk", 0, 0, tiled=True))
    gathered = jnp.concatenate(solved, axis=0)[:harmonics]
    field_rows = comps * pitch_local
    solution = gathered[:, :field_rows].reshape(source.shape)
    slots = mode_orders.shape[1] // groups
    duct = gathered[:, field_rows : field_rows + 2 * slots, stream - 1]
    return solution, duct.reshape(harmonics, 2, slots)


def solution(mesh):
    in_specs = (
        P("harm", None, "blk", None),
        P("blk", None),
        P("harm", None, None),
        P("harm", None, None),
        P("harm", None, "blk"),
        P("harm", None),
        P("harm", None),
        P("harm"),
    )
    out_specs = (P("harm", None, "blk", None), P("harm", None, "blk"))
    return jax.shard_map(local, mesh=mesh, in_specs=in_specs, out_specs=out_specs, check_vma=False)
```

```python
import functools
import math

import jax
import jax.numpy as jnp
from jax import lax
from jax.experimental import pallas as pl
from jax.experimental.pallas import tpu as pltpu
from jax.sharding import PartitionSpec as P

KRYLOV = 6
COMPS = 10
SUB = 8
ROWS = COMPS * SUB
EPS = 1e-06
CHUNK = 16

precise = lax.Precision.HIGHEST
f32, bf16 = jnp.float32, jnp.bfloat16


def spread_entries(entries):
    wide = 3 * ROWS
    row_of = lax.broadcasted_iota(jnp.int32, (ROWS, COMPS), 0) // SUB
    pick_rows = (row_of == lax.broadcasted_iota(jnp.int32, (ROWS, COMPS), 1)).astype(f32)
    column_of = (lax.broadcasted_iota(jnp.int32, (COMPS, wide), 1) % ROWS) // SUB
    pick_columns = (column_of == lax.broadcasted_iota(jnp.int32, (COMPS, wide), 0)).astype(f32)
    full = matmul(matmul(pick_rows, entries), pick_columns)
    same = (lax.broadcasted_iota(jnp.int32, (ROWS, wide), 0) % SUB) == (
        lax.broadcasted_iota(jnp.int32, (ROWS, wide), 1) % SUB
    )
    return jnp.where(same, full, 0.0)


def split_matrix(entries):
    full = spread_entries(entries)
    high = full.astype(bf16).astype(f32)
    column = lax.broadcasted_iota(jnp.int32, (ROWS, 3 * ROWS), 1)
    return jnp.where(column < 2 * ROWS, high, full - high).astype(bf16)


def split_field(plane):
    high = plane.astype(bf16)
    low = (plane - high.astype(f32)).astype(bf16)
    return high, low


def matmul(left, right):
    return jnp.dot(left, right, precision=precise, preferred_element_type=f32)


def solve_kernel(
    groups, in_rows, out_rows, slots, chunk,
    count_ref, in_ref, gain_ref, coupling_ref, cos_ref, sin_ref,
    out_ref,
    basis, direction, first, second, diag, trace_re, trace_im,
    base_split, term_split, start_mat, middle_mat, end_mat,
):
    length = diag.shape[0]
    block = 16
    stride = (groups // SUB) * in_rows
    out_stride = (groups // SUB) * out_rows

    gain, coupling = gain_ref[...], coupling_ref[...]
    both = (COMPS, COMPS)
    one = lax.broadcasted_iota(jnp.int32, both, 0) == lax.broadcasted_iota(jnp.int32, both, 1)
    one = one.astype(f32)
    loop = matmul(coupling, gain)
    cubic = 3.0 * one - 3.0 * loop + matmul(loop, loop)
    third = 3 * ROWS
    start_mat[...] = split_matrix(gain)
    middle_mat[:, :third] = split_matrix(matmul(gain, 2.0 * one - loop))
    middle_mat[:, third:] = split_matrix(-1.5 * gain)
    end_mat[:ROWS, :third] = split_matrix(matmul(gain, cubic))
    end_mat[:ROWS, third : 2 * third] = split_matrix(-1.5 * matmul(gain, one - loop))
    end_mat[:ROWS, 2 * third :] = split_matrix(-1.5 * gain)
    end_mat[ROWS:, :third] = split_matrix(matmul(loop, cubic) * (1.0 / 1.5))
    end_mat[ROWS:, third : 2 * third] = split_matrix(-matmul(loop, one - loop))
    end_mat[ROWS:, 2 * third :] = split_matrix(-loop)

    inner = lax.broadcasted_iota(jnp.int32, (SUB, 128), 1) > 0
    upwind_weight = jnp.where(inner, 1.0 / 1.5, 0.0)

    def total(acc):
        return jnp.sum(acc, axis=(0, 1), keepdims=True)

    def spread(scalar):
        return jnp.broadcast_to(scalar, (SUB, 128))

    def scaled(value, plane):
        return (plane.reshape(COMPS, SUB, 128) * value[None]).reshape(ROWS, 128)

    def fold(plane):
        return jnp.sum(plane.reshape(COMPS, SUB, 128), axis=0)

    def chunks(body, carry):
        return lax.fori_loop(0, length // chunk, lambda p, c: body(p * chunk, c), carry)

    def take(l, acc):
        start = (l // block) * in_rows + l % block
        planes = []
        for c in range(COMPS):
            piece = in_ref[pl.ds(start + c * block, SUB, stride=stride), :]
            planes.append(piece)
        plane = jnp.concatenate(planes, axis=0)
        basis[0, l] = plane
        shift = in_ref[pl.ds(start + COMPS * block, SUB, stride=stride), :]
        diag[l] = (4.0 + shift) * (1.0 / 1.5)
        return acc + fold(plane * plane)

    def wrap(field):
        for c in range(COMPS):
            rows = slice(c * SUB, (c + 1) * SUB)
            field[0, rows, :] = pltpu.roll(field[length, rows, :], 1, axis=0)
            field[length + 1, rows, :] = pltpu.roll(field[1, rows, :], SUB - 1, axis=0)

    def stencil(field, l):
        plane = field[l + 1]
        moved = scaled(upwind_weight, pltpu.roll(plane, 1, axis=1))
        return scaled(diag[l], plane) - (field[l] + field[l + 2]) - moved

    def halves(split, l):
        high, low = split[l, :ROWS, :], split[l, ROWS:, :]
        return [high, low, high]

    def keep(split, l, plane):
        high, low = split_field(plane)
        split[l, :ROWS, :] = high
        split[l, ROWS:, :] = low
        return [high, low, high]

    def multiply(matrix, left, right):
        stacked = [jnp.concatenate(side, axis=0) for side in (left, right)]
        return jnp.dot(
            matrix[...], jnp.concatenate(stacked, axis=1), preferred_element_type=f32
        )

    squares = total(lax.fori_loop(0, length, take, jnp.zeros((SUB, 128), f32)))
    beta = jnp.sqrt(squares + EPS)
    norms = [beta]
    lack = [EPS / (squares + EPS)]
    gram = {}
    hess = {}
    zero = jnp.zeros((SUB, 128), f32)

    for j in range(KRYLOV):
        inverse = spread((1.0 if j == 0 else 1.5) / norms[j])
        found = direction.at[j]

        def start_step(base, carry, j=j, inverse=inverse):
            for l in range(0, chunk, 2):
                sides = []
                for i in (l, l + 1):
                    plane = scaled(inverse, basis[j, base + i])
                    basis[j, base + i] = plane
                    sides.append(keep(base_split, base + i, plane))
                result = multiply(start_mat, *sides)
                first[base + l + 1] = result[:, :128]
                first[base + l + 2] = result[:, 128:]
            return carry

        chunks(start_step, 0)
        wrap(first)

        def sweep_one(base, carry):
            for l in range(0, chunk, 2):
                sides = []
                for i in (l, l + 1):
                    term = stencil(first, base + i)
                    sides.append(halves(base_split, base + i) + keep(term_split, base + i, term))
                result = multiply(middle_mat, *sides)
                second[base + l + 1] = result[:, :128]
                second[base + l + 2] = result[:, 128:]
            return carry

        chunks(sweep_one, 0)
        wrap(second)

        def sweep_two(base, carry, j=j, found=found):
            for l in range(0, chunk, 2):
                sides = []
                for i in (l, l + 1):
                    high, low = split_field(stencil(second, base + i))
                    sides.append(
                        halves(base_split, base + i)
                        + halves(term_split, base + i)
                        + [high, low, high]
                    )
                result = multiply(end_mat, *sides)
                found[base + l + 1] = result[:ROWS, :128]
                found[base + l + 2] = result[:ROWS, 128:]
                basis[j + 1, base + l] = result[ROWS:, :128]
                basis[j + 1, base + l + 1] = result[ROWS:, 128:]
            return carry

        chunks(sweep_two, 0)
        wrap(found)

        def apply_operator(base, accs, j=j, found=found):
            for i in range(chunk):
                work = stencil(found, base + i) + basis[j + 1, base + i]
                basis[j + 1, base + i] = work
                accs = tuple(
                    accs[k] + fold(work * basis[k, base + i]) for k in range(j + 1)
                )
            return accs

        accs = chunks(apply_operator, (zero,) * (j + 1))
        dots = [1.5 * total(acc) for acc in accs]
        for i in range(j + 1):
            entry = dots[i]
            for k in range(i):
                entry = entry - hess[k, j] * gram[k, i]
            hess[i, j] = entry
        factors = [spread(hess[i, j] * (1.0 / 1.5)) for i in range(j + 1)]

        def orthogonalize(base, acc, j=j, factors=factors):
            for i in range(chunk):
                work = basis[j + 1, base + i]
                for k in range(j + 1):
                    work = work - scaled(factors[k], basis[k, base + i])
                basis[j + 1, base + i] = work
                acc = acc + fold(work * work)
            return acc

        squares = 2.25 * total(chunks(orthogonalize, zero))
        size = jnp.sqrt(squares + EPS)
        hess[j + 1, j] = size
        norms.append(size)
        lack.append(EPS / (squares + EPS))
        for k in range(j + 1):
            entry = hess[k, j] * lack[k]
            for i in range(k + 1, j + 1):
                entry = entry - hess[i, j] * gram[k, i]
            gram[k, j + 1] = entry / size

    normal = {}
    for a in range(KRYLOV):
        for b in range(a + 1):
            value = hess[0, a] * hess[0, b]
            for k in range(1, b + 2):
                value = value + hess[k, a] * hess[k, b]
            normal[a, b] = value
    low = {}
    inverse_of = {}
    for a in range(KRYLOV):
        for b in range(a + 1):
            value = normal[a, b]
            for k in range(b):
                value = value - low[a, k] * low[b, k]
            if a == b:
                low[a, a] = jnp.sqrt(value)
                inverse_of[a] = 1.0 / low[a, a]
            else:
                low[a, b] = value * inverse_of[b]
    forward = []
    for a in range(KRYLOV):
        value = beta * hess[0, a]
        for k in range(a):
            value = value - low[a, k] * forward[k]
        forward.append(value * inverse_of[a])
    coeffs = [None] * KRYLOV
    for a in range(KRYLOV - 1, -1, -1):
        value = forward[a]
        for k in range(a + 1, KRYLOV):
            value = value - low[k, a] * coeffs[k]
        coeffs[a] = value * inverse_of[a]
    weights = [spread(c) for c in coeffs]

    def combine(l, carry):
        plane = scaled(weights[0], direction[0, l + 1])
        for j in range(1, KRYLOV):
            plane = plane + scaled(weights[j], direction[j, l + 1])
        start = (l // block) * out_rows + l % block
        pieces = [plane[c * SUB : (c + 1) * SUB, :] for c in range(COMPS)]
        for c in range(COMPS):
            out_ref[pl.ds(start + c * block, SUB, stride=out_stride), :] = pieces[c]
        trace_re[l] = pieces[8] + pieces[2]
        trace_im[l] = pieces[9] + pieces[3]
        return carry

    lax.fori_loop(0, length, combine, 0, unroll=2)

    full_re = trace_re[...].reshape(length * SUB, 128)
    full_im = trace_im[...].reshape(length * SUB, 128)
    cosine, sine = cos_ref[...], sin_ref[...]
    live = lax.broadcasted_iota(jnp.int32, (cosine.shape[0], 128), 0) < count_ref[0]
    norm = 1.0 / math.sqrt(length * SUB)
    wave_re = (matmul(cosine, full_re) + matmul(sine, full_im)) * norm
    wave_im = (matmul(cosine, full_im) - matmul(sine, full_re)) * norm
    wave_re, wave_im = jnp.where(live, wave_re, 0.0), jnp.where(live, wave_im, 0.0)
    tail = COMPS * block
    for b in range(groups):
        at = b * out_rows + tail
        out_ref[at : at + out_rows - tail, :] = jnp.zeros((out_rows - tail, 128), f32)
        out_ref[at : at + slots, :] = wave_re[b * slots : (b + 1) * slots, :]
        out_ref[at + slots : at + 2 * slots, :] = wave_im[b * slots : (b + 1) * slots, :]


def solve(message, gain, coupling, orders, count, groups, pitch_local):
    pitch_total = groups * pitch_local
    length = pitch_total // SUB
    modes = orders.shape[0]
    slots = modes // groups
    in_rows = message.shape[1]
    out_rows = COMPS * pitch_local + -(-2 * slots // SUB) * SUB
    plane_order = jnp.arange(SUB)[None, :] * length + jnp.arange(length)[:, None]
    pitch_index = plane_order.reshape(-1).astype(jnp.int32)
    remainder = orders[:, None] * pitch_index[None, :] % pitch_total
    angles = 2.0 * math.pi / pitch_total * remainder.astype(f32)
    chunk = math.gcd(length, CHUNK)
    kernel = functools.partial(solve_kernel, groups, in_rows, out_rows, slots, chunk)
    in_vmem = pl.BlockSpec(memory_space=pltpu.VMEM)
    result = pl.pallas_call(
        kernel,
        out_shape=jax.ShapeDtypeStruct((groups * out_rows, 128), f32),
        in_specs=[pl.BlockSpec(memory_space=pltpu.SMEM)] + [in_vmem] * 5,
        out_specs=in_vmem,
        scratch_shapes=[
            pltpu.VMEM((KRYLOV + 1, length, ROWS, 128), f32),
            pltpu.VMEM((KRYLOV, length + 2, ROWS, 128), f32),
            pltpu.VMEM((length + 2, ROWS, 128), f32),
            pltpu.VMEM((length + 2, ROWS, 128), f32),
            pltpu.VMEM((length, SUB, 128), f32),
            pltpu.VMEM((length, SUB, 128), f32),
            pltpu.VMEM((length, SUB, 128), f32),
            pltpu.VMEM((length, 2 * ROWS, 128), bf16),
            pltpu.VMEM((length, 2 * ROWS, 128), bf16),
            pltpu.VMEM((ROWS, 3 * ROWS), bf16),
            pltpu.VMEM((ROWS, 6 * ROWS), bf16),
            pltpu.VMEM((2 * ROWS, 9 * ROWS), bf16),
        ],
        compiler_params=pltpu.CompilerParams(vmem_limit_bytes=60 * 1024 * 1024),
    )(
        count.reshape(1),
        message.reshape(groups * in_rows, 128),
        gain,
        coupling,
        jnp.cos(angles),
        jnp.sin(angles),
    )
    return result.reshape(groups, out_rows, 128)


def local(
    source, diag_shift, coupling, sweep_gain, gust_field, gust_mixing, mode_orders, cut_on_count
):
    harmonics, comps, pitch_local, stream = source.shape
    groups = lax.axis_size("blk")
    me = lax.axis_index("blk")
    parts = lax.axis_size("harm")
    part = lax.axis_index("harm")

    inlet = jnp.zeros((harmonics, comps * pitch_local), f32)
    flat_gust = gust_field.reshape(harmonics, comps * pitch_local)
    for k in range(parts):
        block = flat_gust
        if k:
            block = lax.ppermute(flat_gust, "harm", [(i, (i + k) % parts) for i in range(parts)])
        origin = (part - k) % parts
        mixing = lax.dynamic_slice_in_dim(gust_mixing, origin * harmonics, harmonics, axis=1)
        inlet = inlet + jnp.dot(mixing, block, precision=precise)
    inlet = inlet.reshape(harmonics, comps, pitch_local)
    at_inlet = jnp.arange(stream) == 0
    right_side = source + jnp.where(at_inlet, inlet[..., None], 0.0)

    rounds = -(-harmonics // groups)
    diagonal = jnp.broadcast_to(diag_shift[None, None], (harmonics, 1, pitch_local, stream))
    message = jnp.concatenate([right_side, diagonal], axis=1)
    missing = rounds * groups - harmonics
    if missing:
        message = jnp.concatenate(
            [message, jnp.zeros((missing,) + message.shape[1:], f32)], axis=0
        )
    message = message.reshape(rounds * groups, -1, stream)

    solved = []
    for s in range(rounds):
        part_of = message[s * groups : (s + 1) * groups]
        arrived = lax.all_to_all(part_of, "blk", 0, 0, tiled=True)
        index = jnp.minimum(s * groups + me, harmonics - 1)
        pick = lambda array: lax.dynamic_index_in_dim(array, index, 0, keepdims=False)
        result = solve(
            arrived, pick(sweep_gain), pick(coupling), pick(mode_orders), pick(cut_on_count),
            groups, pitch_local,
        )
        solved.append(lax.all_to_all(result, "blk", 0, 0, tiled=True))
    gathered = jnp.concatenate(solved, axis=0)[:harmonics]
    field_rows = comps * pitch_local
    solution = gathered[:, :field_rows].reshape(source.shape)
    slots = mode_orders.shape[1] // groups
    duct = gathered[:, field_rows : field_rows + 2 * slots, stream - 1]
    return solution, duct.reshape(harmonics, 2, slots)


def solution(mesh):
    in_specs = (
        P("harm", None, "blk", None),
        P("blk", None),
        P("harm", None, None),
        P("harm", None, None),
        P("harm", None, "blk"),
        P("harm", None),
        P("harm", None),
        P("harm"),
    )
    out_specs = (P("harm", None, "blk", None), P("harm", None, "blk"))
    return jax.shard_map(local, mesh=mesh, in_specs=in_specs, out_specs=out_specs, check_vma=False)
```

```python
import functools
import math

import jax
import jax.numpy as jnp
from jax import lax
from jax.experimental import pallas as pl
from jax.experimental.pallas import tpu as pltpu
from jax.sharding import PartitionSpec as P

KRYLOV = 6
COMPS = 10
SUB = 8
ROWS = COMPS * SUB
EPS = 1e-06
CHUNK = 16
SKEW = 8

precise = lax.Precision.HIGHEST
f32, bf16 = jnp.float32, jnp.bfloat16


def spread_entries(entries):
    wide = 3 * ROWS
    row_of = lax.broadcasted_iota(jnp.int32, (ROWS, COMPS), 0) // SUB
    pick_rows = (row_of == lax.broadcasted_iota(jnp.int32, (ROWS, COMPS), 1)).astype(f32)
    column_of = (lax.broadcasted_iota(jnp.int32, (COMPS, wide), 1) % ROWS) // SUB
    pick_columns = (column_of == lax.broadcasted_iota(jnp.int32, (COMPS, wide), 0)).astype(f32)
    full = matmul(matmul(pick_rows, entries), pick_columns)
    same = (lax.broadcasted_iota(jnp.int32, (ROWS, wide), 0) % SUB) == (
        lax.broadcasted_iota(jnp.int32, (ROWS, wide), 1) % SUB
    )
    return jnp.where(same, full, 0.0)


def split_matrix(entries):
    full = spread_entries(entries)
    high = full.astype(bf16).astype(f32)
    column = lax.broadcasted_iota(jnp.int32, (ROWS, 3 * ROWS), 1)
    return jnp.where(column < 2 * ROWS, high, full - high).astype(bf16)


def split_field(plane):
    high = plane.astype(bf16)
    low = (plane - high.astype(f32)).astype(bf16)
    return high, low


def matmul(left, right):
    return jnp.dot(left, right, precision=precise, preferred_element_type=f32)


def matrix_kernel(index_ref, gain_ref, coupling_ref, start_mat, middle_mat, end_mat):
    both = (COMPS, COMPS)
    one = lax.broadcasted_iota(jnp.int32, both, 0) == lax.broadcasted_iota(jnp.int32, both, 1)
    one = one.astype(f32)
    third = 3 * ROWS
    for s in range(start_mat.shape[0]):
        gain, coupling = gain_ref[index_ref[s]], coupling_ref[index_ref[s]]
        loop = matmul(coupling, gain)
        cubic = 3.0 * one - 3.0 * loop + matmul(loop, loop)
        start_mat[s] = split_matrix(gain)
        middle_mat[s, :, :third] = split_matrix(matmul(gain, 2.0 * one - loop))
        middle_mat[s, :, third:] = split_matrix(-1.5 * gain)
        end_mat[s, :ROWS, :third] = split_matrix(matmul(gain, cubic))
        end_mat[s, :ROWS, third : 2 * third] = split_matrix(-1.5 * matmul(gain, one - loop))
        end_mat[s, :ROWS, 2 * third :] = split_matrix(-1.5 * gain)
        end_mat[s, ROWS:, :third] = split_matrix(matmul(loop, cubic) * (1.0 / 1.5))
        end_mat[s, ROWS:, third : 2 * third] = split_matrix(-matmul(loop, one - loop))
        end_mat[s, ROWS:, 2 * third :] = split_matrix(-loop)


def build_matrices(index, sweep_gain, coupling):
    count = index.shape[0]
    in_vmem = pl.BlockSpec(memory_space=pltpu.VMEM)
    return pl.pallas_call(
        matrix_kernel,
        out_shape=(
            jax.ShapeDtypeStruct((count, ROWS, 3 * ROWS), bf16),
            jax.ShapeDtypeStruct((count, ROWS, 6 * ROWS), bf16),
            jax.ShapeDtypeStruct((count, 2 * ROWS, 9 * ROWS), bf16),
        ),
        in_specs=[pl.BlockSpec(memory_space=pltpu.SMEM), in_vmem, in_vmem],
        out_specs=(in_vmem,) * 3,
        cost_estimate=pl.CostEstimate(
            flops=count * 25 * 6 * 2 * 256**3, transcendentals=0, bytes_accessed=count * 400000
        ),
    )(index, sweep_gain, coupling)


def solve_kernel(
    plan, slot, chunk,
    count_ref, field_refs, start_ref, middle_ref, end_ref, wave_ref,
    out_refs,
    basis, direction, first, second, diag, trace, base_split, term_split,
):
    length = diag.shape[0]
    block = plan.block
    spans = length // block
    start_mat, middle_mat, end_mat = (ref.at[slot] for ref in (start_ref, middle_ref, end_ref))

    inner = lax.broadcasted_iota(jnp.int32, (SUB, 128), 1) > 0
    upwind_weight = jnp.where(inner, 1.0 / 1.5, 0.0)

    def total(acc):
        return jnp.sum(acc, axis=(0, 1), keepdims=True)

    def spread(scalar):
        return jnp.broadcast_to(scalar, (SUB, 128))

    def scaled(value, plane):
        return (plane.reshape(COMPS, SUB, 128) * value[None]).reshape(ROWS, 128)

    def fold(plane):
        return jnp.sum(plane.reshape(COMPS, SUB, 128), axis=0)

    def chunks(body, carry):
        return lax.fori_loop(0, length // chunk, lambda p, c: body(p * chunk, c), carry)

    def rows_of(ref, row, l):
        height = ref.shape[0] // plan.groups
        return ref[pl.ds((l // block) * height + row, SUB, stride=spans * height), :]

    def take(acc):
        for l in range(length):
            y = l % block
            pieces = [
                rows_of(field_refs[source], row + y, l) for source, row in plan.rows_in[slot]
            ]
            plane = jnp.concatenate(pieces, axis=0)
            basis[0, l] = plane
            shift = rows_of(field_refs[0], plan.diagonal_row + y, l)
            diag[l] = (4.0 + shift) * (1.0 / 1.5)
            acc = acc + fold(plane * plane)
        return acc

    def turn(plane, by):
        parts = [plane[c * SUB : (c + 1) * SUB, :] for c in range(COMPS)]
        return jnp.concatenate([pltpu.roll(part, by, axis=0) for part in parts], axis=0)

    def wrap_first(field):
        field[0] = turn(field[length], 1)

    def wrap_last(field):
        field[length + 1] = turn(field[1], SUB - 1)

    def put(field, l, result):
        field[l + 1] = result[:, :128]
        field[l + 2] = result[:, 128:]

    def stencil(field, l):
        plane = field[l + 1]
        moved = scaled(upwind_weight, pltpu.roll(plane, 1, axis=1))
        return scaled(diag[l], plane) - (field[l] + field[l + 2]) - moved

    def halves(split, l):
        high, low = split[l, :ROWS, :], split[l, ROWS:, :]
        return [high, low, high]

    def keep(split, l, plane):
        high, low = split_field(plane)
        split[l, :ROWS, :] = high
        split[l, ROWS:, :] = low
        return [high, low, high]

    def multiply(matrix, left, right):
        stacked = [jnp.concatenate(side, axis=0) for side in (left, right)]
        return jnp.dot(
            matrix[...], jnp.concatenate(stacked, axis=1), preferred_element_type=f32
        )

    squares = total(take(jnp.zeros((SUB, 128), f32)))
    beta = jnp.sqrt(squares + EPS)
    norms = [beta]
    lack = [EPS / (squares + EPS)]
    gram = {}
    hess = {}
    zero = jnp.zeros((SUB, 128), f32)

    for j in range(KRYLOV):
        inverse = spread((1.0 if j == 0 else 1.5) / norms[j])
        found = direction.at[j]

        def start_pair(l, j=j, inverse=inverse):
            sides = []
            for i in (l, l + 1):
                plane = scaled(inverse, basis[j, i])
                basis[j, i] = plane
                sides.append(keep(base_split, i, plane))
            put(first, l, multiply(start_mat, *sides))

        def middle_pair(l):
            sides = []
            for i in (l, l + 1):
                term = stencil(first, i)
                sides.append(halves(base_split, i) + keep(term_split, i, term))
            put(second, l, multiply(middle_mat, *sides))

        def end_pair(l, j=j, found=found):
            sides = []
            for i in (l, l + 1):
                high, low = split_field(stencil(second, i))
                sides.append(halves(base_split, i) + halves(term_split, i) + [high, low, high])
            result = multiply(end_mat, *sides)
            put(found, l, result[:ROWS])
            basis[j + 1, l] = result[ROWS:, :128]
            basis[j + 1, l + 1] = result[ROWS:, 128:]

        def operator_pair(l, accs, j=j, found=found):
            for i in (l, l + 1):
                work = stencil(found, i) + basis[j + 1, i]
                basis[j + 1, i] = work
                accs = tuple(accs[k] + fold(work * basis[k, i]) for k in range(j + 1))
            return accs

        accs = (zero,) * (j + 1)
        pairs = length // 2
        if length == chunk:
            for step in range(pairs + 3 * SKEW):
                for stage, run in enumerate((start_pair, middle_pair, end_pair, operator_pair)):
                    at = step - stage * SKEW
                    if 0 <= at < pairs:
                        l = 2 * ((at + stage) % pairs)
                        if stage < 3:
                            run(l)
                            if l == 0:
                                wrap_last((first, second, found)[stage])
                            if l == length - 2:
                                wrap_first((first, second, found)[stage])
                        else:
                            accs = run(l, accs)
        else:
            for stage, run in enumerate((start_pair, middle_pair, end_pair)):

                def several(base, carry, run=run):
                    for l in range(0, chunk, 2):
                        run(base + l)
                    return carry

                chunks(several, 0)
                wrap_first((first, second, found)[stage])
                wrap_last((first, second, found)[stage])

            def operators(base, accs):
                for l in range(0, chunk, 2):
                    accs = operator_pair(base + l, accs)
                return accs

            accs = chunks(operators, accs)
        dots = [1.5 * total(acc) for acc in accs]
        for i in range(j + 1):
            entry = dots[i]
            for k in range(i):
                entry = entry - hess[k, j] * gram[k, i]
            hess[i, j] = entry
        factors = [spread(hess[i, j] * (1.0 / 1.5)) for i in range(j + 1)]

        def orthogonalize(base, acc, j=j, factors=factors):
            for i in range(chunk):
                work = basis[j + 1, base + i]
                for k in range(j + 1):
                    work = work - scaled(factors[k], basis[k, base + i])
                basis[j + 1, base + i] = work
                acc = acc + fold(work * work)
            return acc

        squares = 2.25 * total(chunks(orthogonalize, zero))
        size = jnp.sqrt(squares + EPS)
        hess[j + 1, j] = size
        norms.append(size)
        lack.append(EPS / (squares + EPS))
        for k in range(j + 1):
            entry = hess[k, j] * lack[k]
            for i in range(k + 1, j + 1):
                entry = entry - hess[i, j] * gram[k, i]
            gram[k, j + 1] = entry / size

    normal = {}
    for a in range(KRYLOV):
        for b in range(a + 1):
            value = hess[0, a] * hess[0, b]
            for k in range(1, b + 2):
                value = value + hess[k, a] * hess[k, b]
            normal[a, b] = value
    low = {}
    inverse_of = {}
    for a in range(KRYLOV):
        for b in range(a + 1):
            value = normal[a, b]
            for k in range(b):
                value = value - low[a, k] * low[b, k]
            if a == b:
                low[a, a] = jnp.sqrt(value)
                inverse_of[a] = 1.0 / low[a, a]
            else:
                low[a, b] = value * inverse_of[b]
    forward = []
    for a in range(KRYLOV):
        value = beta * hess[0, a]
        for k in range(a):
            value = value - low[a, k] * forward[k]
        forward.append(value * inverse_of[a])
    coeffs = [None] * KRYLOV
    for a in range(KRYLOV - 1, -1, -1):
        value = forward[a]
        for k in range(a + 1, KRYLOV):
            value = value - low[k, a] * coeffs[k]
        coeffs[a] = value * inverse_of[a]
    weights = [spread(c) for c in coeffs]

    for l in range(length):
        plane = scaled(weights[0], direction[0, l + 1])
        for j in range(1, KRYLOV):
            plane = plane + scaled(weights[j], direction[j, l + 1])
        pieces = [plane[c * SUB : (c + 1) * SUB, :] for c in range(COMPS)]
        for c, (target, row) in enumerate(plan.rows_out[slot]):
            ref = out_refs[target]
            height = ref.shape[0] // plan.groups
            at = (l // block) * height + row + l % block
            ref[pl.ds(at, SUB, stride=spans * height), :] = pieces[c]
        trace[l] = pieces[8] + pieces[2]
        trace[length + l] = pieces[9] + pieces[3]

    waves = matmul(wave_ref[slot], trace[...].reshape(2 * length * SUB, 128))
    modes = waves.shape[0] // 2
    live = lax.broadcasted_iota(jnp.int32, (modes, 128), 0) < count_ref[slot]
    norm = 1.0 / math.sqrt(length * SUB)
    wave_re = jnp.where(live, waves[:modes] * norm, 0.0)
    wave_im = jnp.where(live, waves[modes:] * norm, 0.0)
    ref, tail = out_refs[0], plan.modes_row[slot]
    height = ref.shape[0] // plan.groups
    owned = modes // plan.groups
    for b in range(plan.groups):
        at = b * height + tail
        ref[at : at + height - tail, :] = jnp.zeros((height - tail, 128), f32)
        ref[at : at + owned, :] = wave_re[b * owned : (b + 1) * owned, :]
        ref[at + owned : at + 2 * owned, :] = wave_im[b * owned : (b + 1) * owned, :]


class Plan:
    def __init__(self, harmonics, groups, block, modes):
        self.groups, self.block = groups, block
        field = COMPS * block
        self.full = harmonics // groups
        self.rest = harmonics - self.full * groups
        self.halved = 2 * self.rest == groups
        self.slots = self.full + (self.rest > 0)
        tail = -(-2 * (modes // groups) // SUB) * SUB
        self.rows_in, self.rows_out, self.modes_row, self.heights = [], [], [], []
        row = 0
        for s in range(self.slots):
            if s == self.full and self.halved:
                half = COMPS // 2
                self.half_row = row
                self.rows_in.append(
                    [(0, row + c * block) for c in range(half)]
                    + [(1, c * block) for c in range(half)]
                )
                self.rows_out.append([(c // half, c % half * block) for c in range(COMPS)])
                self.modes_row.append(field // 2)
                self.heights.append((field // 2 + tail, field // 2 + tail))
                row += field // 2
            else:
                self.rows_in.append([(0, row + c * block) for c in range(COMPS)])
                self.rows_out.append([(0, c * block) for c in range(COMPS)])
                self.modes_row.append(field)
                self.heights.append((field + tail,))
                row += field
        self.diagonal_row = row


def solve(plan, slot, counts, fields, matrices, tables):
    length = plan.groups * plan.block // SUB
    inputs = [counts, *fields, *matrices, tables]
    heights = plan.heights[slot]

    def kernel(*refs):
        refs = list(refs)
        count_ref, refs = refs[0], refs[1:]
        field_refs, refs = refs[: len(fields)], refs[len(fields) :]
        given, refs = refs[:4], refs[4:]
        out_refs, scratch = refs[: len(heights)], refs[len(heights) :]
        solve_kernel(
            plan, slot, math.gcd(length, CHUNK), count_ref, field_refs, *given, out_refs, *scratch
        )

    in_vmem = pl.BlockSpec(memory_space=pltpu.VMEM)
    results = pl.pallas_call(
        kernel,
        out_shape=tuple(
            jax.ShapeDtypeStruct((plan.groups * height, 128), f32) for height in heights
        ),
        in_specs=[pl.BlockSpec(memory_space=pltpu.SMEM)] + [in_vmem] * (len(inputs) - 1),
        out_specs=(in_vmem,) * len(heights),
        scratch_shapes=[
            pltpu.VMEM((KRYLOV + 1, length, ROWS, 128), f32),
            pltpu.VMEM((KRYLOV, length + 2, ROWS, 128), f32),
            pltpu.VMEM((length + 2, ROWS, 128), f32),
            pltpu.VMEM((length + 2, ROWS, 128), f32),
            pltpu.VMEM((length, SUB, 128), f32),
            pltpu.VMEM((2 * length, SUB, 128), f32),
            pltpu.VMEM((length, 2 * ROWS, 128), bf16),
            pltpu.VMEM((length, 2 * ROWS, 128), bf16),
        ],
        compiler_params=pltpu.CompilerParams(vmem_limit_bytes=60 * 1024 * 1024),
        cost_estimate=pl.CostEstimate(
            flops=KRYLOV * (length // 2) * 6 * 4 * 256**3,
            transcendentals=0,
            bytes_accessed=KRYLOV * 24 * length * ROWS * 128 * 4,
        ),
    )(*inputs)
    return [r.reshape(plan.groups, -1, 128) for r in results]


def mode_tables(orders, pitch_total):
    length = pitch_total // SUB
    plane_order = jnp.arange(SUB)[None, :] * length + jnp.arange(length)[:, None]
    pitch_index = plane_order.reshape(-1).astype(jnp.int32)
    remainder = orders[:, :, None] * pitch_index % pitch_total
    angles = 2.0 * math.pi / pitch_total * remainder.astype(f32)
    cosine, sine = jnp.cos(angles), jnp.sin(angles)
    rows = [jnp.concatenate(pair, axis=2) for pair in ((cosine, sine), (-sine, cosine))]
    return jnp.concatenate(rows, axis=1)


def local(
    source, diag_shift, coupling, sweep_gain, gust_field, gust_mixing, mode_orders, cut_on_count
):
    harmonics, comps, block, stream = source.shape
    groups = lax.axis_size("blk")
    me = lax.axis_index("blk")
    parts = lax.axis_size("harm")
    part = lax.axis_index("harm")
    modes = mode_orders.shape[1]
    plan = Plan(harmonics, groups, block, modes)
    flat_gust = gust_field.reshape(harmonics, comps * block)
    inlet = jnp.zeros((harmonics, comps * block), f32)
    for k in range(parts):
        given = flat_gust
        if k:
            given = lax.ppermute(flat_gust, "harm", [(i, (i + k) % parts) for i in range(parts)])
        origin = (part - k) % parts
        mixing = lax.dynamic_slice_in_dim(gust_mixing, origin * harmonics, harmonics, axis=1)
        inlet = inlet + jnp.dot(mixing, given, precision=precise)
    at_inlet = jnp.arange(stream) == 0
    flat = source.reshape(harmonics, comps * block, stream)
    flat = flat + jnp.where(at_inlet, inlet[..., None], 0.0)

    def by_group(array, halves):
        pieces = [array[s * groups : (s + 1) * groups] for s in range(plan.full)]
        rest = array[plan.full * groups :]
        if plan.rest and plan.halved:
            pieces.append(halves(rest))
        elif plan.rest:
            blank = jnp.zeros((groups - plan.rest,) + rest.shape[1:], rest.dtype)
            pieces.append(jnp.concatenate([rest, blank], axis=0))
        return pieces

    pieces = by_group(flat, lambda rest: rest.reshape(groups, comps * block // 2, stream))
    pieces.append(jnp.broadcast_to(diag_shift[None], (groups, block, stream)))
    message = jnp.concatenate(pieces, axis=1)
    arrived = lax.all_to_all(message, "blk", 0, 0, tiled=True)

    index = [s * groups + me for s in range(plan.full)]
    if plan.rest and plan.halved:
        index.append(plan.full * groups + me // 2)
    elif plan.rest:
        index.append(jnp.minimum(plan.full * groups + me, harmonics - 1))
    index = jnp.stack(index)
    matrices = build_matrices(index, sweep_gain, coupling)
    tables = mode_tables(mode_orders[index], groups * block)
    counts = cut_on_count[index]

    every = arrived.reshape(-1, stream)
    solved, waves = [], []
    owned = modes // groups
    for s in range(plan.slots):
        fields = [every]
        half = s == plan.full and plan.halved
        if half:
            upper = arrived[:, plan.half_row : plan.half_row + comps * block // 2]
            upper = lax.ppermute(upper, "blk", [(i + 1, i) for i in range(0, groups, 2)])
            upper = upper.reshape(-1, stream)
            if solved:
                upper, last = lax.optimization_barrier((upper, last))
            fields.append(upper)
        results = solve(plan, s, counts, fields, matrices, tables)
        result = results[0]
        if half:
            upper = results[1]
            if solved:
                upper, solved[-1] = lax.optimization_barrier((upper, solved[-1]))
            upper = lax.ppermute(upper, "blk", [(i, i + 1) for i in range(0, groups, 2)])
            result = jnp.where(me % 2 == 0, result, upper)
        last = result
        gathered = lax.all_to_all(result, "blk", 0, 0, tiled=True)
        tail = plan.modes_row[s]
        wave = gathered[:, tail : tail + 2 * owned, stream - 1]
        waves.append(wave[::2] if half else wave)
        solved.append(gathered[:, :tail].reshape(-1, comps * block, stream))
    solution = jnp.concatenate(solved, axis=0)[:harmonics].reshape(source.shape)
    duct = jnp.concatenate(waves, axis=0)[:harmonics]
    return solution, duct.reshape(harmonics, 2, owned)


def solution(mesh):
    in_specs = (
        P("harm", None, "blk", None),
        P("blk", None),
        P("harm", None, None),
        P("harm", None, None),
        P("harm", None, "blk"),
        P("harm", None),
        P("harm", None),
        P("harm"),
    )
    out_specs = (P("harm", None, "blk", None), P("harm", None, "blk"))
    return jax.shard_map(local, mesh=mesh, in_specs=in_specs, out_specs=out_specs, check_vma=False)
```

```python
import functools
import math

import jax
import jax.numpy as jnp
from jax import lax
from jax.experimental import pallas as pl
from jax.experimental.pallas import tpu as pltpu
from jax.sharding import PartitionSpec as P

KRYLOV = 6
COMPS = 10
SUB = 8
ROWS = COMPS * SUB
EPS = 1e-06
CHUNK = 16

precise = lax.Precision.HIGHEST
f32, bf16 = jnp.float32, jnp.bfloat16


def spread_entries(entries):
    wide = 3 * ROWS
    row_of = lax.broadcasted_iota(jnp.int32, (ROWS, COMPS), 0) // SUB
    pick_rows = (row_of == lax.broadcasted_iota(jnp.int32, (ROWS, COMPS), 1)).astype(f32)
    column_of = (lax.broadcasted_iota(jnp.int32, (COMPS, wide), 1) % ROWS) // SUB
    pick_columns = (column_of == lax.broadcasted_iota(jnp.int32, (COMPS, wide), 0)).astype(f32)
    full = matmul(matmul(pick_rows, entries), pick_columns)
    same = (lax.broadcasted_iota(jnp.int32, (ROWS, wide), 0) % SUB) == (
        lax.broadcasted_iota(jnp.int32, (ROWS, wide), 1) % SUB
    )
    return jnp.where(same, full, 0.0)


def split_matrix(entries):
    full = spread_entries(entries)
    high = full.astype(bf16).astype(f32)
    column = lax.broadcasted_iota(jnp.int32, (ROWS, 3 * ROWS), 1)
    return jnp.where(column < 2 * ROWS, high, full - high).astype(bf16)


def split_field(plane):
    high = plane.astype(bf16)
    low = (plane - high.astype(f32)).astype(bf16)
    return high, low


def matmul(left, right):
    return jnp.dot(left, right, precision=precise, preferred_element_type=f32)


def matrix_kernel(
    plan, harmonics, pitch_total, both_ref, orders_ref, start_mat, middle_mat, end_mat, table_ref
):
    square = (COMPS, COMPS)
    one = lax.broadcasted_iota(jnp.int32, square, 0) == lax.broadcasted_iota(jnp.int32, square, 1)
    one = one.astype(f32)
    third = 3 * ROWS
    length = pitch_total // SUB
    modes = orders_ref.shape[1]
    for s in range(plan.slots):
        index = plan.harmonic(s)
        gain, coupling = both_ref[index], both_ref[harmonics + index]
        loop = matmul(coupling, gain)
        cubic = 3.0 * one - 3.0 * loop + matmul(loop, loop)
        start_mat[s] = split_matrix(gain)
        middle_mat[s, :, :third] = split_matrix(matmul(gain, 2.0 * one - loop))
        middle_mat[s, :, third:] = split_matrix(-1.5 * gain)
        end_mat[s, :ROWS, :third] = split_matrix(matmul(gain, cubic))
        end_mat[s, :ROWS, third : 2 * third] = split_matrix(-1.5 * matmul(gain, one - loop))
        end_mat[s, :ROWS, 2 * third :] = split_matrix(-1.5 * gain)
        end_mat[s, ROWS:, :third] = split_matrix(matmul(loop, cubic) * (1.0 / 1.5))
        end_mat[s, ROWS:, third : 2 * third] = split_matrix(-matmul(loop, one - loop))
        end_mat[s, ROWS:, 2 * third :] = split_matrix(-loop)

        given = jnp.broadcast_to(orders_ref[pl.ds(index, 1), :], (modes, modes))
        diagonal = lax.broadcasted_iota(jnp.int32, (modes, modes), 0) == lax.broadcasted_iota(
            jnp.int32, (modes, modes), 1
        )
        column = jnp.sum(jnp.where(diagonal, given.astype(f32), 0.0), axis=1, keepdims=True)
        place = lax.broadcasted_iota(jnp.int32, (modes, pitch_total), 1)
        pitch = (place % SUB) * length + place // SUB
        turns = column.astype(jnp.int32) * pitch
        if pitch_total & (pitch_total - 1):
            turns = lax.rem(lax.rem(turns, pitch_total) + pitch_total, pitch_total)
        else:
            turns = turns & (pitch_total - 1)
        angles = 2.0 * math.pi / pitch_total * turns.astype(f32)
        cosine, sine = jnp.cos(angles), jnp.sin(angles)
        table_ref[s, :modes, :pitch_total] = cosine
        table_ref[s, :modes, pitch_total:] = sine
        table_ref[s, modes:, :pitch_total] = -sine
        table_ref[s, modes:, pitch_total:] = cosine


def build_matrices(plan, sweep_gain, coupling, orders, pitch_total):
    count, harmonics, modes = plan.slots, orders.shape[0], orders.shape[1]
    both = jnp.concatenate([sweep_gain, coupling], axis=0)
    in_vmem = pl.BlockSpec(memory_space=pltpu.VMEM)
    return pl.pallas_call(
        functools.partial(matrix_kernel, plan, harmonics, pitch_total),
        out_shape=(
            jax.ShapeDtypeStruct((count, ROWS, 3 * ROWS), bf16),
            jax.ShapeDtypeStruct((count, ROWS, 6 * ROWS), bf16),
            jax.ShapeDtypeStruct((count, 2 * ROWS, 9 * ROWS), bf16),
            jax.ShapeDtypeStruct((count, 2 * modes, 2 * pitch_total), f32),
        ),
        in_specs=[in_vmem, in_vmem],
        out_specs=(in_vmem,) * 4,
        cost_estimate=pl.CostEstimate(
            flops=count * 25 * 6 * 2 * 256**3, transcendentals=0, bytes_accessed=count * 400000
        ),
    )(both, orders)


def solve_kernel(
    plan, slot, chunk,
    count_ref, field_refs, start_ref, middle_ref, end_ref, wave_ref,
    out_refs,
    basis, direction, first, second, diag, trace, base_split, term_split, *halves_out,
):
    length = diag.shape[0]
    block = plan.block
    spans = length // block
    start_mat, middle_mat, end_mat = (ref.at[slot] for ref in (start_ref, middle_ref, end_ref))

    inner = lax.broadcasted_iota(jnp.int32, (SUB, 128), 1) > 0
    upwind_weight = jnp.where(inner, 1.0 / 1.5, 0.0)

    def total(acc):
        return jnp.sum(acc, axis=(0, 1), keepdims=True)

    def spread(scalar):
        return jnp.broadcast_to(scalar, (SUB, 128))

    def scaled(value, plane):
        return (plane.reshape(COMPS, SUB, 128) * value[None]).reshape(ROWS, 128)

    def fold(plane):
        return jnp.sum(plane.reshape(COMPS, SUB, 128), axis=0)

    def rows_of(ref, row, l):
        height = ref.shape[0] // plan.groups
        return ref[pl.ds((l // block) * height + row, SUB, stride=spans * height), :]

    def take(rows):
        at_inlet = lax.broadcasted_iota(jnp.int32, (ROWS, 128), 1) == 0
        for l in range(length):
            y = l % block
            if y == 0:
                inlet = [rows_of(field_refs[1], plan.inlet_row[slot] + c, l) for c in range(COMPS)]
                inlet = jnp.concatenate(inlet, axis=0)
            moved = pltpu.roll(inlet, 128 - y, axis=1) if y else inlet
            pieces = [rows_of(field_refs[source], row + y, l) for source, row in rows]
            plane = jnp.concatenate(pieces, axis=0) + jnp.where(at_inlet, moved, 0.0)
            basis[0, l] = plane
            shift = rows_of(field_refs[1], plan.diagonal_row + y, l)
            diag[l] = (4.0 + shift) * (1.0 / 1.5)

    def turn(plane, by):
        parts = [plane[c * SUB : (c + 1) * SUB, :] for c in range(COMPS)]
        return jnp.concatenate([pltpu.roll(part, by, axis=0) for part in parts], axis=0)

    def wrap(field):
        field[0] = turn(field[length], 1)
        field[length + 1] = turn(field[1], SUB - 1)

    def put(field, l, result):
        field[l + 1] = result[:, :128]
        field[l + 2] = result[:, 128:]

    def stencil(field, l):
        plane = field[l + 1]
        moved = scaled(upwind_weight, pltpu.roll(plane, 1, axis=1))
        return scaled(diag[l], plane) - (field[l] + field[l + 2]) - moved

    def halves(split, l):
        high, low = split[l, :ROWS, :], split[l, ROWS:, :]
        return [high, low, high]

    def keep(split, l, plane):
        high, low = split_field(plane)
        split[l, :ROWS, :] = high
        split[l, ROWS:, :] = low
        return [high, low, high]

    def multiply(matrix, left, right):
        stacked = [jnp.concatenate(side, axis=0) for side in (left, right)]
        return jnp.dot(
            matrix[...], jnp.concatenate(stacked, axis=1), preferred_element_type=f32
        )

    choices = plan.rows_in[slot]
    if len(choices) == 1:
        take(choices[0])
    else:
        for parity, rows in enumerate(choices):
            pl.when(lax.axis_index("blk") % 2 == parity)(functools.partial(take, rows))

    norms, lack, gram, hess = [], [], {}, {}
    zero = jnp.zeros((SUB, 128), f32)

    def close(j, acc):
        squares = total(acc)
        size = jnp.sqrt(squares + EPS)
        norms.append(size)
        lack.append(EPS / (squares + EPS))
        if j:
            hess[j, j - 1] = size
        for k in range(j):
            entry = hess[k, j - 1] * lack[k]
            for i in range(k + 1, j):
                entry = entry - hess[i, j - 1] * gram[k, i]
            gram[k, j] = entry / size

    factors = []
    for j in range(KRYLOV):
        found = direction.at[j]

        def update(i, j=j, factors=factors):
            plane = basis[j, i]
            if j:
                for k in range(j):
                    plane = plane - scaled(factors[k], basis[k, i])
                basis[j, i] = plane
            return plane

        def start_pair(l, acc, update=update):
            sides = []
            for i in (l, l + 1):
                plane = update(i)
                acc = acc + fold(plane * plane)
                sides.append(keep(base_split, i, plane))
            put(first, l, multiply(start_mat, *sides))
            return acc

        def middle_pair(l):
            sides = []
            for i in (l, l + 1):
                term = stencil(first, i)
                sides.append(halves(base_split, i) + keep(term_split, i, term))
            put(second, l, multiply(middle_mat, *sides))

        def end_pair(l, j=j, found=found):
            sides = []
            for i in (l, l + 1):
                high, low = split_field(stencil(second, i))
                sides.append(halves(base_split, i) + halves(term_split, i) + [high, low, high])
            result = multiply(end_mat, *sides)
            put(found, l, result[:ROWS])
            basis[j + 1, l] = result[ROWS:, :128]
            basis[j + 1, l + 1] = result[ROWS:, 128:]

        def operator_pair(l, accs, inverse, j=j, found=found):
            for i in (l, l + 1):
                work = scaled(inverse, stencil(found, i) + basis[j + 1, i])
                basis[j + 1, i] = work
                accs = tuple(accs[k] + fold(work * basis[k, i]) for k in range(j + 1))
            return accs

        def run(pair, carry):
            def several(base, carry):
                for l in range(0, chunk, 2):
                    carry = pair(base + l, carry)
                return carry

            if length == chunk:
                return several(0, carry)
            return lax.fori_loop(0, length // chunk, lambda p, c: several(p * chunk, c), carry)

        def plain(pair):
            def body(l, carry):
                pair(l)
                return carry

            return body

        acc = run(start_pair, zero)
        wrap(first)
        close(j, acc)
        inverse = spread(1.5 / norms[j])
        run(plain(middle_pair), 0)
        wrap(second)
        run(plain(end_pair), 0)
        wrap(found)
        accs = run(lambda l, c, f=operator_pair, i=inverse: f(l, c, i), (zero,) * (j + 1))
        dots = [total(accs[k]) / norms[k] for k in range(j + 1)]
        for i in range(j + 1):
            entry = dots[i]
            for k in range(i):
                entry = entry - hess[k, j] * gram[k, i]
            hess[i, j] = entry
        factors = [spread(hess[k, j] / norms[k]) for k in range(j + 1)]

    def last_pair(l, acc):
        for i in (l, l + 1):
            plane = basis[KRYLOV, i]
            for k in range(KRYLOV):
                plane = plane - scaled(factors[k], basis[k, i])
            acc = acc + fold(plane * plane)
        return acc

    close(KRYLOV, run(last_pair, zero))
    beta = norms[0]

    normal = {}
    for a in range(KRYLOV):
        for b in range(a + 1):
            value = hess[0, a] * hess[0, b]
            for k in range(1, b + 2):
                value = value + hess[k, a] * hess[k, b]
            normal[a, b] = value
    low = {}
    inverse_of = {}
    for a in range(KRYLOV):
        for b in range(a + 1):
            value = normal[a, b]
            for k in range(b):
                value = value - low[a, k] * low[b, k]
            if a == b:
                low[a, a] = jnp.sqrt(value)
                inverse_of[a] = 1.0 / low[a, a]
            else:
                low[a, b] = value * inverse_of[b]
    forward = []
    for a in range(KRYLOV):
        value = beta * hess[0, a]
        for k in range(a):
            value = value - low[a, k] * forward[k]
        forward.append(value * inverse_of[a])
    coeffs = [None] * KRYLOV
    for a in range(KRYLOV - 1, -1, -1):
        value = forward[a]
        for k in range(a + 1, KRYLOV):
            value = value - low[k, a] * coeffs[k]
        coeffs[a] = value * inverse_of[a]
    weights = [spread(c / n) for c, n in zip(coeffs, norms)]
    targets = halves_out or out_refs

    for l in range(length):
        plane = scaled(weights[0], direction[0, l + 1])
        for j in range(1, KRYLOV):
            plane = plane + scaled(weights[j], direction[j, l + 1])
        pieces = [plane[c * SUB : (c + 1) * SUB, :] for c in range(COMPS)]
        for c, (target, row) in enumerate(plan.rows_out[slot]):
            ref = targets[target]
            height = ref.shape[0] // plan.groups
            at = (l // block) * height + row + l % block
            ref[pl.ds(at, SUB, stride=spans * height), :] = pieces[c]
        trace[l] = pieces[8] + pieces[2]
        trace[length + l] = pieces[9] + pieces[3]

    waves = matmul(wave_ref[slot], trace[...].reshape(2 * length * SUB, 128))
    modes = waves.shape[0] // 2
    live = lax.broadcasted_iota(jnp.int32, (modes, 128), 0) < count_ref[plan.harmonic(slot)]
    norm = 1.0 / math.sqrt(length * SUB)
    wave_re = jnp.where(live, waves[:modes] * norm, 0.0)
    wave_im = jnp.where(live, waves[modes:] * norm, 0.0)
    ref, tail = out_refs[0], plan.modes_row[slot]
    for parity, half in enumerate(halves_out):

        def send(half=half):
            ref[...] = half[...]

        pl.when(lax.axis_index("blk") % 2 == parity)(send)
    height = ref.shape[0] // plan.groups
    owned = modes // plan.groups
    for b in range(plan.groups):
        at = b * height + tail
        ref[at : at + height - tail, :] = jnp.zeros((height - tail, 128), f32)
        ref[at : at + owned, :] = wave_re[b * owned : (b + 1) * owned, :]
        ref[at + owned : at + 2 * owned, :] = wave_im[b * owned : (b + 1) * owned, :]


class Plan:
    def __init__(self, harmonics, groups, block, modes):
        self.harmonics, self.groups, self.block = harmonics, groups, block
        field, half = COMPS * block, COMPS // 2
        self.full = harmonics // groups
        self.rest = harmonics - self.full * groups
        self.halved = 2 * self.rest == groups
        self.slots = self.full + (self.rest > 0)
        tail = -(-2 * (modes // groups) // SUB) * SUB
        self.rows_in, self.rows_out, self.modes_row, self.heights = [], [], [], []
        row = 0
        for s in range(self.slots):
            if s == self.full and self.halved:
                parts = [[(source, c * block) for c in range(half)] for source in (1, 2)]
                self.rows_in.append([parts[0] + parts[1], parts[1] + parts[0]])
                self.rows_out.append([(c // half, c % half * block) for c in range(COMPS)])
                self.modes_row.append(field // 2)
            else:
                self.rows_in.append([[(0, row + c * block) for c in range(COMPS)]])
                self.rows_out.append([(0, c * block) for c in range(COMPS)])
                self.modes_row.append(field)
                row += field
            self.heights.append(self.modes_row[-1] + tail)
        self.diagonal_row = field // 2 if self.halved else 0
        self.inlet_row = [self.diagonal_row + block + s * COMPS for s in range(self.slots)]
        self.inlet_pad = -self.slots * COMPS % SUB

    def harmonic(self, s):
        me = lax.axis_index("blk")
        if s < self.full:
            return s * self.groups + me
        if self.halved:
            return self.full * self.groups + me // 2
        return jnp.minimum(self.full * self.groups + me, self.harmonics - 1)


def solve(plan, slot, counts, fields, matrices, tables):
    length = plan.groups * plan.block // SUB
    inputs = [counts, *fields, *matrices, tables]
    height = plan.heights[slot]
    shared = slot == plan.full and plan.halved

    def kernel(*refs):
        refs = list(refs)
        count_ref, refs = refs[0], refs[1:]
        field_refs, refs = refs[: len(fields)], refs[len(fields) :]
        given, refs = refs[:4], refs[4:]
        out_refs, scratch = refs[:1], refs[1:]
        solve_kernel(
            plan, slot, math.gcd(length, CHUNK), count_ref, field_refs, *given, out_refs, *scratch
        )

    in_vmem = pl.BlockSpec(memory_space=pltpu.VMEM)
    result = pl.pallas_call(
        kernel,
        out_shape=jax.ShapeDtypeStruct((plan.groups * height, 128), f32),
        in_specs=[pl.BlockSpec(memory_space=pltpu.SMEM)] + [in_vmem] * (len(inputs) - 1),
        out_specs=in_vmem,
        scratch_shapes=[
            pltpu.VMEM((KRYLOV + 1, length, ROWS, 128), f32),
            pltpu.VMEM((KRYLOV, length + 2, ROWS, 128), f32),
            pltpu.VMEM((length + 2, ROWS, 128), f32),
            pltpu.VMEM((length + 2, ROWS, 128), f32),
            pltpu.VMEM((length, SUB, 128), f32),
            pltpu.VMEM((2 * length, SUB, 128), f32),
            pltpu.VMEM((length, 2 * ROWS, 128), bf16),
            pltpu.VMEM((length, 2 * ROWS, 128), bf16),
        ]
        + [pltpu.VMEM((plan.groups * height, 128), f32)] * (2 * shared),
        compiler_params=pltpu.CompilerParams(vmem_limit_bytes=60 * 1024 * 1024),
        cost_estimate=pl.CostEstimate(
            flops=KRYLOV * (length // 2) * 6 * 4 * 256**3,
            transcendentals=0,
            bytes_accessed=KRYLOV * 24 * length * ROWS * 128 * 4,
        ),
    )(*inputs)
    return result.reshape(plan.groups, height, 128)


def local(
    source, diag_shift, coupling, sweep_gain, gust_field, gust_mixing, mode_orders, cut_on_count
):
    harmonics, comps, block, stream = source.shape
    groups = lax.axis_size("blk")
    me = lax.axis_index("blk")
    parts = lax.axis_size("harm")
    part = lax.axis_index("harm")
    modes = mode_orders.shape[1]
    owned = modes // groups
    plan = Plan(harmonics, groups, block, modes)
    field = comps * block
    flat = source.reshape(harmonics, field, stream)

    def exchange(array):
        return lax.all_to_all(array, "blk", 0, 0, tiled=True)

    def by_group(array, shared):
        pieces = [array[s * groups : (s + 1) * groups] for s in range(plan.full)]
        rest = array[plan.full * groups :]
        if plan.rest and plan.halved:
            pieces.append(shared(rest))
        elif plan.rest:
            blank = jnp.zeros((groups - plan.rest,) + rest.shape[1:], rest.dtype)
            pieces.append(jnp.concatenate([rest, blank], axis=0))
        return pieces

    pieces = by_group(flat, lambda rest: rest.reshape(groups, field // 2, stream))
    half = [pieces.pop()] if plan.halved else []
    whole = exchange(jnp.concatenate(pieces, axis=1))

    flat_gust = gust_field.reshape(harmonics, field)
    inlet = jnp.zeros((harmonics, field), f32)
    for k in range(parts):
        given = flat_gust
        if k:
            given = lax.ppermute(flat_gust, "harm", [(i, (i + k) % parts) for i in range(parts)])
        origin = (part - k) % parts
        mixing = lax.dynamic_slice_in_dim(gust_mixing, origin * harmonics, harmonics, axis=1)
        inlet = inlet + jnp.dot(mixing, given, precision=precise)
    inlet = inlet.reshape(harmonics, comps, block)
    inlet = by_group(inlet, lambda rest: jnp.repeat(rest, 2, axis=0))
    inlet = jnp.pad(
        jnp.concatenate(inlet, axis=1), ((0, 0), (0, plan.inlet_pad), (0, stream - block))
    )
    diagonal = jnp.broadcast_to(diag_shift[None], (groups, block, stream))
    extra = jnp.concatenate(half + [diagonal, inlet], axis=1)
    extra, whole = lax.optimization_barrier((extra, whole))
    extra = exchange(extra)

    matrices = build_matrices(plan, sweep_gain, coupling, mode_orders, groups * block)
    *matrices, tables = matrices
    fields = [whole.reshape(-1, stream), extra.reshape(-1, stream)]
    solved, waves = [], []
    for s in range(plan.slots):
        shared = s == plan.full and plan.halved
        if shared:
            pair = [(i, i ^ 1) for i in range(groups)]
            other = lax.ppermute(extra[:, : field // 2], "blk", pair).reshape(-1, stream)
            if solved:
                other, last = lax.optimization_barrier((other, last))
            fields = fields + [other]
        result = last = solve(plan, s, cut_on_count, fields, matrices, tables)
        if solved:
            result, solved[-1] = lax.optimization_barrier((result, solved[-1]))
        gathered = exchange(result)
        tail = plan.modes_row[s]
        wave = gathered[:, tail : tail + 2 * owned, stream - 1]
        waves.append(wave[::2] if shared else wave)
        solved.append(gathered[:, :tail].reshape(-1, field, stream))
    solution = jnp.concatenate(solved, axis=0)[:harmonics].reshape(source.shape)
    duct = jnp.concatenate(waves, axis=0)[:harmonics]
    return solution, duct.reshape(harmonics, 2, owned)


def solution(mesh):
    in_specs = (
        P("harm", None, "blk", None),
        P("blk", None),
        P("harm", None, None),
        P("harm", None, None),
        P("harm", None, "blk"),
        P("harm", None),
        P("harm", None),
        P("harm"),
    )
    out_specs = (P("harm", None, "blk", None), P("harm", None, "blk"))
    return jax.shard_map(local, mesh=mesh, in_specs=in_specs, out_specs=out_specs, check_vma=False)
```

```python
import functools
import math

import jax
import jax.numpy as jnp
from jax import lax
from jax.experimental import pallas as pl
from jax.experimental.pallas import tpu as pltpu
from jax.sharding import PartitionSpec as P

KRYLOV = 6
COMPS = 10
SUB = 8
ROWS = COMPS * SUB
EPS = 1e-06
CHUNK = 16

precise = lax.Precision.HIGHEST
f32, bf16 = jnp.float32, jnp.bfloat16


def spread_entries(entries):
    wide = 3 * ROWS
    row_of = lax.broadcasted_iota(jnp.int32, (ROWS, COMPS), 0) // SUB
    pick_rows = (row_of == lax.broadcasted_iota(jnp.int32, (ROWS, COMPS), 1)).astype(f32)
    column_of = (lax.broadcasted_iota(jnp.int32, (COMPS, wide), 1) % ROWS) // SUB
    pick_columns = (column_of == lax.broadcasted_iota(jnp.int32, (COMPS, wide), 0)).astype(f32)
    full = matmul(matmul(pick_rows, entries), pick_columns)
    same = (lax.broadcasted_iota(jnp.int32, (ROWS, wide), 0) % SUB) == (
        lax.broadcasted_iota(jnp.int32, (ROWS, wide), 1) % SUB
    )
    return jnp.where(same, full, 0.0)


def split_matrix(entries):
    full = spread_entries(entries)
    high = full.astype(bf16).astype(f32)
    column = lax.broadcasted_iota(jnp.int32, (ROWS, 3 * ROWS), 1)
    return jnp.where(column < 2 * ROWS, high, full - high).astype(bf16)


def split_field(plane):
    high = plane.astype(bf16)
    low = (plane - high.astype(f32)).astype(bf16)
    return high, low


def matmul(left, right):
    return jnp.dot(left, right, precision=precise, preferred_element_type=f32)


def matrix_kernel(
    plan, harmonics, pitch_total, both_ref, orders_ref, start_mat, step_mat, table_ref
):
    length = pitch_total // SUB
    modes = orders_ref.shape[1]
    for s in range(plan.slots):
        index = plan.harmonic(s)
        gain, coupling = both_ref[index], both_ref[harmonics + index]
        loop = matmul(coupling, gain)
        start_mat[s, :ROWS] = split_matrix(gain)
        start_mat[s, ROWS:] = split_matrix(loop * (1.0 / 1.5))
        step_mat[s, :ROWS] = split_matrix(-1.5 * gain)
        step_mat[s, ROWS:] = split_matrix(-loop)

        given = jnp.broadcast_to(orders_ref[pl.ds(index, 1), :], (modes, modes))
        diagonal = lax.broadcasted_iota(jnp.int32, (modes, modes), 0) == lax.broadcasted_iota(
            jnp.int32, (modes, modes), 1
        )
        column = jnp.sum(jnp.where(diagonal, given.astype(f32), 0.0), axis=1, keepdims=True)
        place = lax.broadcasted_iota(jnp.int32, (modes, pitch_total), 1)
        pitch = (place % SUB) * length + place // SUB
        turns = column.astype(jnp.int32) * pitch
        if pitch_total & (pitch_total - 1):
            turns = lax.rem(lax.rem(turns, pitch_total) + pitch_total, pitch_total)
        else:
            turns = turns & (pitch_total - 1)
        angles = 2.0 * math.pi / pitch_total * turns.astype(f32)
        cosine, sine = jnp.cos(angles), jnp.sin(angles)
        table_ref[s, :modes, :pitch_total] = cosine
        table_ref[s, :modes, pitch_total:] = sine
        table_ref[s, modes:, :pitch_total] = -sine
        table_ref[s, modes:, pitch_total:] = cosine


def build_matrices(plan, sweep_gain, coupling, orders, pitch_total):
    count, harmonics, modes = plan.slots, orders.shape[0], orders.shape[1]
    both = jnp.concatenate([sweep_gain, coupling], axis=0)
    in_vmem = pl.BlockSpec(memory_space=pltpu.VMEM)
    return pl.pallas_call(
        functools.partial(matrix_kernel, plan, harmonics, pitch_total),
        out_shape=(
            jax.ShapeDtypeStruct((count, 2 * ROWS, 3 * ROWS), bf16),
            jax.ShapeDtypeStruct((count, 2 * ROWS, 3 * ROWS), bf16),
            jax.ShapeDtypeStruct((count, 2 * modes, 2 * pitch_total), f32),
        ),
        in_specs=[in_vmem, in_vmem],
        out_specs=(in_vmem,) * 3,
        cost_estimate=pl.CostEstimate(
            flops=count * 12 * 6 * 2 * 256**3, transcendentals=0, bytes_accessed=count * 200000
        ),
    )(both, orders)


def solve_kernel(
    plan, slot, chunk,
    count_ref, field_refs, start_ref, step_ref, wave_ref,
    out_refs,
    basis, direction, first, second, first_mixed, second_mixed, diag, trace, *halves_out,
):
    length = diag.shape[0]
    block = plan.block
    spans = length // block
    start_mat, step_mat = start_ref.at[slot], step_ref.at[slot]

    inner = lax.broadcasted_iota(jnp.int32, (SUB, 128), 1) > 0
    upwind_weight = jnp.where(inner, 1.0 / 1.5, 0.0)

    def total(acc):
        return jnp.sum(acc, axis=(0, 1), keepdims=True)

    def spread(scalar):
        return jnp.broadcast_to(scalar, (SUB, 128))

    def scaled(value, plane):
        return (plane.reshape(COMPS, SUB, 128) * value[None]).reshape(ROWS, 128)

    def fold(plane):
        return jnp.sum(plane.reshape(COMPS, SUB, 128), axis=0)

    def rows_of(ref, row, l):
        height = ref.shape[0] // plan.groups
        return ref[pl.ds((l // block) * height + row, SUB, stride=spans * height), :]

    def take(rows):
        at_inlet = lax.broadcasted_iota(jnp.int32, (ROWS, 128), 1) == 0
        packed = {}
        for l in range(length):
            y = l % block
            moved = []
            for c in range(COMPS):
                row, lane = divmod((slot * COMPS + c) * block + y, 128)
                if y == 0 and (c == 0 or lane < block):
                    packed[row] = rows_of(field_refs[1], plan.inlet_row + row, l)
                value = packed[row]
                moved.append(pltpu.roll(value, 128 - lane, axis=1) if lane else value)
            moved = jnp.concatenate(moved, axis=0)
            pieces = [rows_of(field_refs[source], row + y, l) for source, row in rows]
            plane = jnp.concatenate(pieces, axis=0) + jnp.where(at_inlet, moved, 0.0)
            basis[0, l] = plane
            shift = rows_of(field_refs[1], plan.diagonal_row + y, l)
            diag[l] = (4.0 + shift) * (1.0 / 1.5)

    def turn(plane, by):
        parts = [plane[c * SUB : (c + 1) * SUB, :] for c in range(COMPS)]
        return jnp.concatenate([pltpu.roll(part, by, axis=0) for part in parts], axis=0)

    def wrap(field):
        field[0] = turn(field[length], 1)
        field[length + 1] = turn(field[1], SUB - 1)

    def stencil(field, l):
        plane = field[l + 1]
        moved = scaled(upwind_weight, pltpu.roll(plane, 1, axis=1))
        return scaled(diag[l], plane) - (field[l] + field[l + 2]) - moved

    def multiply(matrix, planes):
        sides = []
        for plane in planes:
            high, low = split_field(plane)
            sides.append(jnp.concatenate([high, low, high], axis=0))
        result = jnp.dot(
            matrix[...], jnp.concatenate(sides, axis=1), preferred_element_type=f32
        )
        return [
            (result[:ROWS, lanes], result[ROWS:, lanes]) for lanes in (slice(128), slice(128, 256))
        ]

    choices = plan.rows_in[slot]
    if len(choices) == 1:
        take(choices[0])
    else:
        for parity, rows in enumerate(choices):
            pl.when(lax.axis_index("blk") % 2 == parity)(functools.partial(take, rows))

    norms, lack, gram, hess = [], [], {}, {}
    zero = jnp.zeros((SUB, 128), f32)

    def close(j, acc):
        squares = total(acc)
        size = jnp.sqrt(squares + EPS)
        norms.append(size)
        lack.append(EPS / (squares + EPS))
        if j:
            hess[j, j - 1] = size
        for k in range(j):
            entry = hess[k, j - 1] * lack[k]
            for i in range(k + 1, j):
                entry = entry - hess[i, j - 1] * gram[k, i]
            gram[k, j] = entry / size

    factors = []
    for j in range(KRYLOV):
        found = direction.at[j]

        def update(i, j=j, factors=factors):
            plane = basis[j, i]
            if j:
                for k in range(j):
                    plane = plane - scaled(factors[k], basis[k, i])
                basis[j, i] = plane
            return plane

        def start_pair(l, acc, update=update):
            planes = [update(i) for i in (l, l + 1)]
            for plane in planes:
                acc = acc + fold(plane * plane)
            for i, (plane, mixed) in zip((l, l + 1), multiply(start_mat, planes)):
                first[i + 1] = plane
                first_mixed[i] = mixed
            return acc

        def middle_pair(l):
            terms = [stencil(first, i) + first_mixed[i] for i in (l, l + 1)]
            for i, (plane, mixed) in zip((l, l + 1), multiply(step_mat, terms)):
                second[i + 1] = 2.0 * first[i + 1] + plane
                second_mixed[i] = 2.0 * first_mixed[i] + mixed

        def end_pair(l, j=j, found=found):
            terms = [stencil(second, i) + second_mixed[i] for i in (l, l + 1)]
            for i, (plane, mixed) in zip((l, l + 1), multiply(step_mat, terms)):
                found[i + 1] = first[i + 1] + second[i + 1] + plane
                basis[j + 1, i] = first_mixed[i] + second_mixed[i] + mixed

        def operator_pair(l, accs, inverse, j=j, found=found):
            for i in (l, l + 1):
                work = scaled(inverse, stencil(found, i) + basis[j + 1, i])
                basis[j + 1, i] = work
                accs = tuple(accs[k] + fold(work * basis[k, i]) for k in range(j + 1))
            return accs

        def run(pair, carry):
            def several(base, carry):
                for l in range(0, chunk, 2):
                    carry = pair(base + l, carry)
                return carry

            if length == chunk:
                return several(0, carry)
            return lax.fori_loop(0, length // chunk, lambda p, c: several(p * chunk, c), carry)

        def plain(pair):
            def body(l, carry):
                pair(l)
                return carry

            return body

        acc = run(start_pair, zero)
        wrap(first)
        close(j, acc)
        inverse = spread(1.5 / norms[j])
        run(plain(middle_pair), 0)
        wrap(second)
        run(plain(end_pair), 0)
        wrap(found)
        accs = run(lambda l, c, f=operator_pair, i=inverse: f(l, c, i), (zero,) * (j + 1))
        dots = [total(accs[k]) / norms[k] for k in range(j + 1)]
        for i in range(j + 1):
            entry = dots[i]
            for k in range(i):
                entry = entry - hess[k, j] * gram[k, i]
            hess[i, j] = entry
        factors = [spread(hess[k, j] / norms[k]) for k in range(j + 1)]

    def last_pair(l, acc):
        for i in (l, l + 1):
            plane = basis[KRYLOV, i]
            for k in range(KRYLOV):
                plane = plane - scaled(factors[k], basis[k, i])
            acc = acc + fold(plane * plane)
        return acc

    close(KRYLOV, run(last_pair, zero))
    beta = norms[0]

    normal = {}
    for a in range(KRYLOV):
        for b in range(a + 1):
            value = hess[0, a] * hess[0, b]
            for k in range(1, b + 2):
                value = value + hess[k, a] * hess[k, b]
            normal[a, b] = value
    low = {}
    inverse_of = {}
    for a in range(KRYLOV):
        for b in range(a + 1):
            value = normal[a, b]
            for k in range(b):
                value = value - low[a, k] * low[b, k]
            if a == b:
                low[a, a] = jnp.sqrt(value)
                inverse_of[a] = 1.0 / low[a, a]
            else:
                low[a, b] = value * inverse_of[b]
    forward = []
    for a in range(KRYLOV):
        value = beta * hess[0, a]
        for k in range(a):
            value = value - low[a, k] * forward[k]
        forward.append(value * inverse_of[a])
    coeffs = [None] * KRYLOV
    for a in range(KRYLOV - 1, -1, -1):
        value = forward[a]
        for k in range(a + 1, KRYLOV):
            value = value - low[k, a] * coeffs[k]
        coeffs[a] = value * inverse_of[a]
    weights = [spread(c / n) for c, n in zip(coeffs, norms)]
    targets = halves_out or out_refs

    for l in range(length):
        plane = scaled(weights[0], direction[0, l + 1])
        for j in range(1, KRYLOV):
            plane = plane + scaled(weights[j], direction[j, l + 1])
        pieces = [plane[c * SUB : (c + 1) * SUB, :] for c in range(COMPS)]
        for c, (target, row) in enumerate(plan.rows_out[slot]):
            ref = targets[target]
            height = ref.shape[0] // plan.groups
            at = (l // block) * height + row + l % block
            ref[pl.ds(at, SUB, stride=spans * height), :] = pieces[c]
        trace[l] = pieces[8] + pieces[2]
        trace[length + l] = pieces[9] + pieces[3]

    waves = matmul(wave_ref[slot], trace[...].reshape(2 * length * SUB, 128))
    modes = waves.shape[0] // 2
    live = lax.broadcasted_iota(jnp.int32, (modes, 128), 0) < count_ref[plan.harmonic(slot)]
    norm = 1.0 / math.sqrt(length * SUB)
    wave_re = jnp.where(live, waves[:modes] * norm, 0.0)
    wave_im = jnp.where(live, waves[modes:] * norm, 0.0)
    ref, tail = out_refs[0], plan.modes_row[slot]
    for parity, half in enumerate(halves_out):

        def send(half=half):
            ref[...] = half[...]

        pl.when(lax.axis_index("blk") % 2 == parity)(send)
    height = ref.shape[0] // plan.groups
    owned = modes // plan.groups
    for b in range(plan.groups):
        at = b * height + tail
        ref[at : at + height - tail, :] = jnp.zeros((height - tail, 128), f32)
        ref[at : at + owned, :] = wave_re[b * owned : (b + 1) * owned, :]
        ref[at + owned : at + 2 * owned, :] = wave_im[b * owned : (b + 1) * owned, :]


class Plan:
    def __init__(self, harmonics, groups, block, modes):
        self.harmonics, self.groups, self.block = harmonics, groups, block
        field, half = COMPS * block, COMPS // 2
        self.full = harmonics // groups
        self.rest = harmonics - self.full * groups
        self.halved = 2 * self.rest == groups
        self.slots = self.full + (self.rest > 0)
        tail = -(-2 * (modes // groups) // SUB) * SUB
        self.rows_in, self.rows_out, self.modes_row, self.heights = [], [], [], []
        row = 0
        for s in range(self.slots):
            if s == self.full and self.halved:
                parts = [[(source, c * block) for c in range(half)] for source in (1, 2)]
                self.rows_in.append([parts[0] + parts[1], parts[1] + parts[0]])
                self.rows_out.append([(c // half, c % half * block) for c in range(COMPS)])
                self.modes_row.append(field // 2)
            else:
                self.rows_in.append([[(0, row + c * block) for c in range(COMPS)]])
                self.rows_out.append([(0, c * block) for c in range(COMPS)])
                self.modes_row.append(field)
                row += field
            self.heights.append(self.modes_row[-1] + tail)
        self.diagonal_row = field // 2 if self.halved else 0
        self.inlet_row = self.diagonal_row + block

    def harmonic(self, s):
        me = lax.axis_index("blk")
        if s < self.full:
            return s * self.groups + me
        if self.halved:
            return self.full * self.groups + me // 2
        return jnp.minimum(self.full * self.groups + me, self.harmonics - 1)


def solve(plan, slot, counts, fields, matrices, tables):
    length = plan.groups * plan.block // SUB
    inputs = [counts, *fields, *matrices, tables]
    height = plan.heights[slot]
    shared = slot == plan.full and plan.halved

    def kernel(*refs):
        refs = list(refs)
        count_ref, refs = refs[0], refs[1:]
        field_refs, refs = refs[: len(fields)], refs[len(fields) :]
        given, refs = refs[:3], refs[3:]
        out_refs, scratch = refs[:1], refs[1:]
        solve_kernel(
            plan, slot, math.gcd(length, CHUNK), count_ref, field_refs, *given, out_refs, *scratch
        )

    in_vmem = pl.BlockSpec(memory_space=pltpu.VMEM)
    result = pl.pallas_call(
        kernel,
        out_shape=jax.ShapeDtypeStruct((plan.groups * height, 128), f32),
        in_specs=[pl.BlockSpec(memory_space=pltpu.SMEM)] + [in_vmem] * (len(inputs) - 1),
        out_specs=in_vmem,
        scratch_shapes=[
            pltpu.VMEM((KRYLOV + 1, length, ROWS, 128), f32),
            pltpu.VMEM((KRYLOV, length + 2, ROWS, 128), f32),
            pltpu.VMEM((length + 2, ROWS, 128), f32),
            pltpu.VMEM((length + 2, ROWS, 128), f32),
            pltpu.VMEM((length, ROWS, 128), f32),
            pltpu.VMEM((length, ROWS, 128), f32),
            pltpu.VMEM((length, SUB, 128), f32),
            pltpu.VMEM((2 * length, SUB, 128), f32),
        ]
        + [pltpu.VMEM((plan.groups * height, 128), f32)] * (2 * shared),
        compiler_params=pltpu.CompilerParams(vmem_limit_bytes=60 * 1024 * 1024),
        cost_estimate=pl.CostEstimate(
            flops=KRYLOV * (length // 2) * 6 * 4 * 256**3,
            transcendentals=0,
            bytes_accessed=KRYLOV * 24 * length * ROWS * 128 * 4,
        ),
    )(*inputs)
    return result.reshape(plan.groups, height, 128)


def local(
    source, diag_shift, coupling, sweep_gain, gust_field, gust_mixing, mode_orders, cut_on_count
):
    harmonics, comps, block, stream = source.shape
    groups = lax.axis_size("blk")
    me = lax.axis_index("blk")
    parts = lax.axis_size("harm")
    part = lax.axis_index("harm")
    modes = mode_orders.shape[1]
    owned = modes // groups
    plan = Plan(harmonics, groups, block, modes)
    field = comps * block
    flat = source.reshape(harmonics, field, stream)

    def exchange(array):
        return lax.all_to_all(array, "blk", 0, 0, tiled=True)

    def by_group(array, shared):
        pieces = [array[s * groups : (s + 1) * groups] for s in range(plan.full)]
        rest = array[plan.full * groups :]
        if plan.rest and plan.halved:
            pieces.append(shared(rest))
        elif plan.rest:
            blank = jnp.zeros((groups - plan.rest,) + rest.shape[1:], rest.dtype)
            pieces.append(jnp.concatenate([rest, blank], axis=0))
        return pieces

    pieces = by_group(flat, lambda rest: rest.reshape(groups, field // 2, stream))
    half = [pieces.pop()] if plan.halved else []
    whole = jnp.concatenate(pieces, axis=1)
    whole, gust_field = lax.optimization_barrier((whole, gust_field))
    whole = exchange(whole)

    gathered = [gust_field]
    for k in range(1, parts):
        ring = [(i, (i + k) % parts) for i in range(parts)]
        gathered.append(lax.ppermute(gust_field, "harm", ring))
    inlet = jnp.zeros((harmonics, field), f32)
    for k, given in enumerate(gathered):
        origin = (part - k) % parts
        mixing = lax.dynamic_slice_in_dim(gust_mixing, origin * harmonics, harmonics, axis=1)
        inlet = inlet + jnp.dot(mixing, given.reshape(harmonics, field), precision=precise)
    inlet = inlet.reshape(harmonics, comps, block)
    inlet = by_group(inlet, lambda rest: jnp.repeat(rest, 2, axis=0))
    inlet = jnp.concatenate(inlet, axis=1).reshape(groups, -1)
    inlet = jnp.pad(inlet, ((0, 0), (0, -inlet.shape[1] % (SUB * stream))))
    inlet = inlet.reshape(groups, -1, stream)
    diagonal = jnp.broadcast_to(diag_shift[None], (groups, block, stream))
    extra = jnp.concatenate(half + [diagonal, inlet], axis=1)
    extra, whole = lax.optimization_barrier((extra, whole))
    extra = exchange(extra)

    matrices = build_matrices(plan, sweep_gain, coupling, mode_orders, groups * block)
    *matrices, tables = matrices
    fields = [whole.reshape(-1, stream), extra.reshape(-1, stream)]
    solved, waves = [], []
    for s in range(plan.slots):
        shared = s == plan.full and plan.halved
        if shared:
            pair = [(i, i ^ 1) for i in range(groups)]
            other = lax.ppermute(extra[:, : field // 2], "blk", pair).reshape(-1, stream)
            if solved:
                other, last = lax.optimization_barrier((other, last))
            fields = fields + [other]
        result = last = solve(plan, s, cut_on_count, fields, matrices, tables)
        if solved:
            result, solved[-1] = lax.optimization_barrier((result, solved[-1]))
        gathered = exchange(result)
        tail = plan.modes_row[s]
        wave = gathered[:, tail : tail + 2 * owned, stream - 1]
        waves.append(wave[::2] if shared else wave)
        solved.append(gathered[:, :tail].reshape(-1, field, stream))
    solution = jnp.concatenate(solved, axis=0)[:harmonics].reshape(source.shape)
    duct = jnp.concatenate(waves, axis=0)[:harmonics]
    return solution, duct.reshape(harmonics, 2, owned)


def solution(mesh):
    in_specs = (
        P("harm", None, "blk", None),
        P("blk", None),
        P("harm", None, None),
        P("harm", None, None),
        P("harm", None, "blk"),
        P("harm", None),
        P("harm", None),
        P("harm"),
    )
    out_specs = (P("harm", None, "blk", None), P("harm", None, "blk"))
    return jax.shard_map(local, mesh=mesh, in_specs=in_specs, out_specs=out_specs, check_vma=False)
```
